256 devices in a mesh: dp: 2 (over y_lo), fsdp: 16 (over z, core), ctx: 8 (over x, y_hi).
Axes of the slice: x: 4, y: 4 (y_hi: 2, y_lo: 2; y = y_hi * 2 + y_lo), z: 8, core: 2. Of those that a mesh axis runs over, the one named last changes fastest.
Arguments:
- inputs: bfloat16 [32, 1024, 16384], P(('dp', 'fsdp'), 'ctx'), may hold values from -14.5 to 14.5
- cotangent: bfloat16 [32, 1024, 2048], P(('dp', 'fsdp'), 'ctx'), may hold values from -5 to 5
- lengths: int32 [32], P(('dp', 'fsdp')), may hold values from 1 to 1024, as said below
- frozen: bfloat16 [16384, 2048], P(('fsdp', 'ctx')), may hold values from -0.125 to 0.125
- adapter_down: bfloat16 [16, 16384], replicated
- adapter_up: bfloat16 [16, 2048], replicated
Outputs:
- input_grads: bfloat16 [32, 1024, 16384], P(('dp', 'fsdp'), 'ctx')
- grad_down: float32 [16, 16384], replicated
- grad_up: float32 [16, 2048], replicated
The draws below stay inside these ranges and needn't reach their ends.
Inputs may be any that keep to these rules, and one draw needn't show every extreme that they name: `lengths`: positions below an example's length are real tokens, the rest padding; some example has all 1024 positions live.
All inputs are finite; a program needn't handle non-finite values.
Results may differ from the reference program's by a relative error of at most 0.0033.
Values may be sent and summed in bfloat16 or wider, within the bound.
A program may use at most 128 MiB of HBM per device.

```python
import math
import jax
import jax.numpy as jnp
from jax import lax

D = 16384
R = 16
OUT = 2048
LENGTH = 1024
EXAMPLES = 32


def scaled_draw(key, dims_shape, scale_axis, lowest, highest):
    jitter_key = jax.random.fold_in(key, 3)
    spread_key = jax.random.fold_in(key, 5)
    scale_count = dims_shape[scale_axis]
    jitter = jnp.clip(jax.random.normal(jitter_key, dims_shape, jnp.float32), -4.0, 4.0)
    spread = jax.random.uniform(spread_key, (scale_count,), jnp.float32, math.log(lowest), math.log(highest))
    target = [1] * len(dims_shape)
    target[scale_axis] = scale_count
    return jitter * jnp.exp(spread).reshape(tuple(target))


def draw_inputs(key, part):
    return scaled_draw(key, (EXAMPLES, LENGTH, D), 2, 0.3, 3.0).astype(jnp.bfloat16)


def draw_cotangent(key, part):
    return scaled_draw(key, (EXAMPLES, LENGTH, OUT), 2, 0.1, 1.0).astype(jnp.bfloat16)


def draw_adapter_down(key, part):
    return (scaled_draw(key, (R, D), 0, 0.3, 3.0) / math.sqrt(D)).astype(jnp.bfloat16)


def draw_adapter_up(key, part):
    return (scaled_draw(key, (R, OUT), 0, 0.3, 3.0) / math.sqrt(OUT)).astype(jnp.bfloat16)


def draw_lengths(key, part):
    order_rank = jax.random.permutation(jax.random.fold_in(key, 11), EXAMPLES)
    bin_width = LENGTH // EXAMPLES
    upper = LENGTH * (order_rank + 1) // EXAMPLES
    offset = jax.random.randint(jax.random.fold_in(key, 13), (EXAMPLES,), 0, bin_width, jnp.int32)
    offset = jnp.where(order_rank == EXAMPLES - 1, 0, offset)
    return (upper - offset).astype(jnp.int32)


def steps_of(stream_key, extent, cuts, smallest, largest):
    factor_of = 1.0
    for dim, shards_of in cuts:
        draws = jax.random.uniform(jax.random.fold_in(jax.random.fold_in(stream_key, 6), dim), (shards_of,), jnp.float32, smallest / len(cuts), largest / len(cuts))
        factor_of = factor_of * jnp.repeat(jnp.exp(draws), extent[dim] // shards_of).reshape((-1,) + (1,) * (len(extent) - 1 - dim))
    return factor_of


def gaussian(rng, shape, deviation, reach, split=(), kind=jnp.bfloat16):
    level = steps_of(rng, shape, split, -0.22, 0.18) if split else 1.0
    drawn = jax.random.normal(rng, shape, jnp.float32) * deviation * level
    return jnp.minimum(jnp.maximum(drawn, -reach), reach).astype(kind)


def setup_inputs(seed: int = 0) -> dict:
    splits = jax.random.split(jax.random.key(seed), 7)
    return {
        "inputs": draw_inputs(jax.random.fold_in(splits[6], 71), 0),
        "cotangent": draw_cotangent(jax.random.fold_in(splits[6], 71), 0),
        "lengths": draw_lengths(jax.random.fold_in(splits[6], 71), 0),
        "frozen": gaussian(splits[3], (D, OUT), OUT ** -0.5, 0.125, ((0, 128),)),
        "adapter_down": draw_adapter_down(jax.random.fold_in(splits[6], 71), 0),
        "adapter_up": draw_adapter_up(jax.random.fold_in(splits[6], 71), 0),
    }


scaling = 2.0

def contract_last(operand, second):
    return lax.dot_general(operand, second, (((1,), (1,)), ((), ())), preferred_element_type=jnp.float32)

def contract_first(operand, second):
    return lax.dot_general(operand, second, (((0,), (0,)), ((), ())), preferred_element_type=jnp.float32)

def reference(inputs, cotangent, lengths, frozen, adapter_down, adapter_up):
    clip_bound = 10.0 * math.sqrt(R * (D + OUT))
    position = jnp.arange(LENGTH, dtype=jnp.int32)

    def per_example(carry, example):
        tokens_in, grads_out, length_now = example
        live_mask = (position < length_now)[:, None]
        masked = jnp.where(live_mask, grads_out, jnp.zeros((), grads_out.dtype))
        lowered = contract_last(masked, adapter_up).astype(jnp.bfloat16)
        projected = contract_last(tokens_in, adapter_down).astype(jnp.bfloat16)
        input_grads = (contract_last(masked, frozen) + scaling * jnp.dot(lowered, adapter_down, preferred_element_type=jnp.float32)).astype(jnp.bfloat16)
        example_down = scaling * contract_first(lowered, tokens_in)
        example_up = scaling * contract_first(projected, masked)
        squared = jnp.sum(example_down * example_down) + jnp.sum(example_up * example_up)
        factor = clip_bound / jnp.maximum(jnp.sqrt(squared), clip_bound)
        sum_down, sum_up = carry
        return ((sum_down + factor * example_down, sum_up + factor * example_up), input_grads)
    initial = (jnp.zeros((R, D), jnp.float32), jnp.zeros((R, OUT), jnp.float32))
    (sum_down, sum_up), input_grads = lax.scan(per_example, initial, (inputs, cotangent, lengths))
    return (input_grads, sum_down / EXAMPLES, sum_up / EXAMPLES)
```

```python
import functools
import math

import jax
import jax.numpy as jnp
from jax import lax
from jax.experimental import pallas as pl
from jax.experimental.pallas import tpu as pltpu
from jax.sharding import PartitionSpec as P

MESH = pl.DeviceIdType.MESH
BF16, F32 = jnp.bfloat16, jnp.float32
X, Z = 4, 8
OFFSETS = (0, -1, 1, -2, 2, -3, 3, 4)
SEMS = dict(
    local=6, tok=4, tok2=2, mate=7, zp=7, zm=7, cross=8, pair=8, out=64,
    s1=1, s2=3, s3=7, s4=1, s5=7, s6=1, s7=7, s8=3, s9=1, s10=1,
)
BASE, TOTAL = {}, 0
for _name, _count in SEMS.items():
    BASE[_name] = TOTAL
    TOTAL += _count


def last(a, b):
    return lax.dot_general(a, b, (((1,), (1,)), ((), ())), preferred_element_type=F32)


def wrap(value, size):
    return lax.rem(value + size, size)


def body(
    lengths, inp, cot, frz, adn, aup,
    og, gd, gu,
    tok, wts, outs, xin, dn, up, low2,
    part, r1, r2, share, nrm, r4, g8, r5, fin, r6, c7, c8, c9, c10,
    ssem, rsem,
):
    dp, fsdp, ctx = (lax.axis_index(n) for n in ("dp", "fsdp", "ctx"))
    lo, z, c, x, hi = dp, fsdp // 2, lax.rem(fsdp, 2), ctx // 2, lax.rem(ctx, 2)
    rows, width = cot.shape
    half = rows // 2

    def dev(dx=0, dz=0, dc=0, flip_hi=0, flip_lo=0):
        xx, zz = wrap(x + dx, X), wrap(z + dz, Z)
        cc = 1 - c if dc else c
        hh = 1 - hi if flip_hi else hi
        ll = 1 - lo if flip_lo else lo
        return (ll, zz * 2 + cc, xx * 2 + hh)

    peers = [dict(dx=dx, dc=dc) for dx in range(X) for dc in range(2) if dx or dc]
    peers += [dict(dz=dz) for dz in range(1, Z)]
    peers += [dict(dx=dx, flip_hi=1) for dx in range(X)]
    peers += [dict(flip_hi=1, flip_lo=1), dict(flip_lo=1)]

    sent = []

    def send(src, dst, name, i, **to):
        s = BASE[name] + i
        copy = pltpu.make_async_remote_copy(
            src, dst, ssem.at[s], rsem.at[s], device_id=dev(**to), device_id_type=MESH
        )
        copy.start()
        sent.append(copy)

    def got(dst, name, i):
        s = BASE[name] + i
        pltpu.make_async_remote_copy(
            dst, dst, ssem.at[s], rsem.at[s], device_id=dev(dc=1), device_id_type=MESH
        ).wait_recv()

    def local(src, dst, i):
        copy = pltpu.make_async_copy(src, dst, rsem.at[BASE["local"] + i])
        copy.start()
        return copy

    own = x * 2 + c

    def slot(dx, dc=0):
        return wrap(x + dx, X) * 2 + (1 - c if dc else c)

    def wz(d):
        return wrap(z + d, Z)

    cot2, frz2 = cot.reshape(2, half, width), frz.reshape(2, half, width)

    loads = [
        local(aup, up, 0),
        local(cot2, tok.at[own], 1),
        local(adn, dn, 2),
        local(inp, xin, 3),
        local(frz2, wts.at[z, hi], 4),
    ]
    barrier = pltpu.get_barrier_semaphore()
    for p in peers:
        pl.semaphore_signal(barrier, inc=1, device_id=dev(**p), device_id_type=MESH)
    pl.semaphore_wait(barrier, len(peers))

    send(cot2.at[0], tok.at[own, 0], "tok", 0, dx=1)
    send(cot2.at[1], tok.at[own, 1], "tok", 3, dx=-1)
    send(frz2.at[lo], wts.at[z, hi, lo], "zp", 0, dz=1)
    send(frz2.at[lo], wts.at[z, hi, lo], "zm", 0, dz=-1)
    send(frz2.at[lo], wts.at[z, hi, lo], "cross", 0, flip_hi=1, flip_lo=1)
    send(cot2.at[1], tok.at[own, 1], "tok", 1, dx=1)
    send(cot2.at[0], tok.at[own, 0], "tok", 2, dx=-1)
    send(frz2.at[1 - lo], wts.at[z, hi, 1 - lo], "zp", 1, dz=1)
    send(frz2.at[1 - lo], wts.at[z, hi, 1 - lo], "zm", 1, dz=-1)
    send(cot2, tok.at[own], "mate", 0, dc=1)

    def partials():
        for copy in loads[:4]:
            copy.wait()
        position = ctx * rows + lax.broadcasted_iota(jnp.int32, (1, rows), 1)
        live = position < lengths[0]
        mine = tok[own].reshape(rows, width)
        lowered = jnp.where(live, last(up[...], mine), 0.0).astype(BF16)
        proj = jnp.where(live, last(dn[...], xin[...]), 0.0).astype(BF16)
        for j in range(2 * X):
            dcol, ucol = xin.shape[1] // (2 * X), width // (2 * X)
            pd = jnp.dot(lowered, xin[:, j * dcol : (j + 1) * dcol], preferred_element_type=F32)
            part[j % 2, j // 2, :, :dcol] = 2.0 * pd
            pu = jnp.dot(proj, mine[:, j * ucol : (j + 1) * ucol], preferred_element_type=F32)
            part[j % 2, j // 2, :, dcol:] = 2.0 * pu
        send(part.at[1 - hi], r1, "s1", 0, flip_hi=1)

    def stage2():
        got(r1, "s1", 0)
        r1[...] = part[hi] + r1[...]
        for dx in range(1, X):
            send(r1.at[wrap(x + dx, X)], r2.at[dx - 1], "s2", dx - 1, dx=dx)

    def stage3():
        for dx in range(1, X):
            got(r2.at[dx - 1], "s2", dx - 1)
        total = r1[x] + r2[0] + r2[1] + r2[2]
        n = total.shape[1] // 2
        share[0] = total[:, :n]
        share[1] = total[:, n:]
        square = jnp.sum(jnp.sum(total * total, axis=1, keepdims=True), axis=0, keepdims=True)
        nrm[ctx] = jnp.broadcast_to(square, nrm.shape[1:])
        for i in range(1, 2 * X):
            send(nrm.at[ctx], nrm.at[ctx], "s3", i - 1, dx=i // 2, flip_hi=i % 2)

    def stage4():
        for i in range(1, 2 * X):
            src = wrap(x - i // 2, X) * 2 + (1 - hi if i % 2 else hi)
            got(nrm.at[src], "s3", i - 1)
        square = nrm[0]
        for i in range(1, 2 * X):
            square = square + nrm[i]
        bound = 10.0 * math.sqrt(dn.shape[0] * (xin.shape[1] + width))
        factor = (bound / jnp.maximum(jnp.sqrt(square), bound))[:1, :1]
        share[...] = share[...] * factor.reshape(1, 1, 1)
        send(share.at[1 - c], r4, "s4", 0, dc=1)

    def stage5():
        got(r4, "s4", 0)
        both = share[c] + r4[...]
        n = g8.shape[2]
        for o in range(Z):
            if o < 6:
                g8[o] = both[(o % 2) * 8 : (o % 2) * 8 + 8, (o // 2) * n : (o // 2 + 1) * n]
            else:
                g8[o] = jnp.zeros(g8.shape[1:], F32)
        for dz in range(1, Z):
            send(g8.at[wz(dz)], r5.at[dz - 1], "s5", dz - 1, dz=dz)

    def stage6():
        total = g8[z]
        for dz in range(1, Z):
            got(r5.at[dz - 1], "s5", dz - 1)
            total = total + r5[dz - 1]
        fin[...] = total
        send(fin, r6, "s6", 0, flip_lo=1)

    def stage7():
        got(r6, "s6", 0)
        c7[z] = (fin[...] + r6[...]) * (1.0 / 32.0)
        for dz in range(1, Z):
            send(c7.at[z], c7.at[z], "s7", dz - 1, dz=dz)

    def stage8():
        for dz in range(1, Z):
            got(c7.at[wz(-dz)], "s7", dz - 1)
        c8[x] = c7[...]
        for dx in range(1, X):
            send(c7, c8.at[x], "s8", dx - 1, dx=dx)

    def stage9():
        for dx in range(1, X):
            got(c8.at[wrap(x - dx, X)], "s8", dx - 1)
        c9[hi] = c8[...]
        send(c8, c9.at[hi], "s9", 0, flip_hi=1, flip_lo=1)

    def stage10():
        got(c9.at[1 - hi], "s9", 0)
        c10[c] = c9[...]
        send(c9, c10.at[c], "s10", 0, dc=1)

    def finish():
        got(c10.at[1 - c], "s10", 0)
        n = g8.shape[2]
        dcol, ucol = xin.shape[1] // (2 * X), width // (2 * X)
        for j in range(2 * X):
            for cc in range(2):
                for o in range(6):
                    r = slice((o % 2) * 8, (o % 2) * 8 + 8)
                    v = c10[cc, j % 2, j // 2, o]
                    at = cc * 3 * n + (o // 2) * n
                    k = max(0, min(n, dcol - at))
                    if k:
                        gd[r, j * dcol + at : j * dcol + at + k] = v[:, :k]
                    if k < n:
                        u = at + k - dcol
                        gu[r, j * ucol + u : j * ucol + u + n - k] = v[:, k:]

    def weights(k):
        d, which = (k + 1) // 2, (lo if k % 2 else 1 - lo)
        at = wts.at[wz(-d), hi, which]
        got(at, "zp", k - 1)
        if k <= 5:
            send(at, at, "zp", k + 1, dz=1)
        if k % 2:
            send(at, at, "cross", OFFSETS.index(-d if d < 4 else 4), flip_hi=1, flip_lo=1)
        if k == 7:
            which = 1 - lo
        at = wts.at[wz(d), hi, which]
        got(at, "zm", k - 1)
        if k <= 4:
            send(at, at, "zm", k + 1, dz=-1)
        if k == 6:
            send(at, at, "zm", 6, dz=-1)
        if k % 2 and k < 7:
            send(at, at, "cross", OFFSETS.index(d), flip_hi=1, flip_lo=1)

    def across(k):
        at = wts.at[wz(OFFSETS[k - 1]), 1 - hi, 1 - lo]
        got(at, "cross", k - 1)
        send(at, at, "pair", k - 1, flip_lo=1)

    def tokens(k):
        if k == 3:
            moved = ((slot(2), 0, "tok2", 0), (slot(2), 1, "tok2", 1))
        else:
            a, b = (0, 1) if k == 1 else (1, 0)
            moved = ((slot(-1), a, "tok", a), (slot(1), b, "tok", 2 + b))
        for i, (s, part_, name, index) in enumerate(moved):
            at = tok.at[s, part_]
            got(at, name, index)
            if k == 1:
                send(at, at, "tok2", i, dx=1 if i == 0 else -1)
            send(at, at, "mate", 1 + 2 * (k - 1) + i, dc=1)

    def all_tokens():
        got(tok.at[slot(0, 1)], "mate", 0)
        for k in range(1, 4):
            a, b = ((slot(-1, 1), 0), (slot(1, 1), 1)) if k == 1 else ((slot(-1, 1), 1), (slot(1, 1), 0))
            if k == 3:
                a, b = (slot(2, 1), 0), (slot(2, 1), 1)
            got(tok.at[a[0], a[1]], "mate", 1 + 2 * (k - 1))
            got(tok.at[b[0], b[1]], "mate", 2 + 2 * (k - 1))

        @pl.loop(0, 4)
        def _(m):
            t = tok[pl.ds(m * 2, 2)].reshape(2 * rows, width)
            lowered = last(t, up[...]).astype(BF16)
            low2[m] = lowered + lowered

    kept = []

    def product(i):
        if i == 1:
            loads[4].wait()
        got(wts.at[wz(OFFSETS[i - 1]), 1 - hi, lo], "pair", i - 1)
        shard = wz(OFFSETS[i - 1])
        wide = 2 * rows
        at = pl.multiple_of(((shard * 2 + c) * 8 + x * 2) * rows, wide)
        cols = pl.ds(at, wide)
        w = wts.at[shard]

        @pl.loop(0, 4)
        def _(m):
            t = tok[pl.ds(m * 2, 2)].reshape(2 * rows, width)
            value = last(t, w[...].reshape(wide, width))
            value = value + jnp.dot(low2[m], dn[:, cols], preferred_element_type=F32)
            outs[i - 1, pl.ds(m * 2, 2)] = value.astype(BF16).reshape(2, rows, wide)

        for dx in (2, 1, 3, 0):
            for dc in range(2):
                src = outs.at[i - 1, slot(dx, dc)]
                if dx or dc:
                    send(src, og.at[:, cols], "out", (i - 1) * 8 + dx * 2 + dc, dx=dx, dc=dc)
                else:
                    copy = pltpu.make_async_copy(
                        src, og.at[:, cols], rsem.at[BASE["out"] + (i - 1) * 8]
                    )
                    copy.start()
                    kept.append(copy)

    def landed(i):
        shard = wz(OFFSETS[i - 1])
        for dx in range(X):
            for dc in range(2):
                if dx or dc:
                    cc = 1 - c if dc else c
                    at = pl.multiple_of(
                        ((shard * 2 + cc) * 8 + wrap(x - dx, X) * 2) * rows, 2 * rows
                    )
                    got(og.at[:, pl.ds(at, 2 * rows)], "out", (i - 1) * 8 + dx * 2 + dc)

    partials()
    gradients = {2: stage2, 3: stage3, 4: stage4, 5: stage5, 6: stage6, 7: stage7, 8: stage8, 9: stage9}
    for k in range(1, 10):
        if k <= 7:
            weights(k)
        if k <= 8:
            across(k)
        if k <= 3:
            tokens(k)
        if k == 3:
            all_tokens()
            product(1)
        if k >= 3:
            product(k - 1)
        if k in gradients:
            gradients[k]()
    stage10()
    finish()
    for i in range(1, 9):
        landed(i)
    for copy in kept:
        copy.wait()
    for copy in sent:
        copy.wait_send()


def fused(lengths, inp, cot, frz, adn, aup):
    rows, width = cot.shape
    rank, features = adn.shape
    share = (features + width) // (2 * X)
    n = share // 6
    scratch = [
        pltpu.VMEM((2 * X, 2, rows // 2, width), BF16),
        pltpu.VMEM((Z, 2, 2, rows // 2, width), BF16),
        pltpu.VMEM((Z, 2 * X, rows, 2 * rows), BF16),
        pltpu.VMEM((rows, features), BF16),
        pltpu.VMEM((rank, features), BF16),
        pltpu.VMEM((rank, width), BF16),
        pltpu.VMEM((4, 2 * rows, rank), BF16),
        pltpu.VMEM((2, X, rank, share), F32),
        pltpu.VMEM((X, rank, share), F32),
        pltpu.VMEM((X - 1, rank, share), F32),
        pltpu.VMEM((2, rank, share // 2), F32),
        pltpu.VMEM((2 * X, 8, 128), F32),
        pltpu.VMEM((rank, share // 2), F32),
        pltpu.VMEM((Z, 8, n), F32),
        pltpu.VMEM((Z - 1, 8, n), F32),
        pltpu.VMEM((8, n), F32),
        pltpu.VMEM((8, n), F32),
        pltpu.VMEM((Z, 8, n), F32),
        pltpu.VMEM((X, Z, 8, n), F32),
        pltpu.VMEM((2, X, Z, 8, n), F32),
        pltpu.VMEM((2, 2, X, Z, 8, n), F32),
        pltpu.SemaphoreType.DMA((TOTAL,)),
        pltpu.SemaphoreType.DMA((TOTAL,)),
    ]
    anywhere = pl.BlockSpec(memory_space=pl.ANY)
    vmem = pl.BlockSpec(memory_space=pltpu.VMEM)
    return pl.pallas_call(
        body,
        out_shape=(
            jax.ShapeDtypeStruct((rows, features), BF16),
            jax.ShapeDtypeStruct((rank, features), F32),
            jax.ShapeDtypeStruct((rank, width), F32),
        ),
        in_specs=[pl.BlockSpec(memory_space=pltpu.SMEM)] + [anywhere] * 5,
        out_specs=(anywhere, vmem, vmem),
        scratch_shapes=scratch,
        compiler_params=pltpu.CompilerParams(
            collective_id=0, has_side_effects=True, vmem_limit_bytes=56 << 20
        ),
    )(lengths, inp, cot, frz, adn, aup)


def shard(inputs, cotangent, lengths, frozen, adapter_down, adapter_up):
    _, rows, features = inputs.shape
    raw, grad_down, grad_up = fused(
        lengths, inputs[0], cotangent[0], frozen, adapter_down, adapter_up
    )
    position = lax.axis_index("ctx") * rows + jnp.arange(rows, dtype=jnp.int32)
    live = position[:, None] < lengths
    input_grads = jnp.where(live, raw, jnp.zeros((), BF16))
    return input_grads[None], grad_down, grad_up


def solution(mesh):
    rows = P(("dp", "fsdp"), "ctx", None)
    return jax.shard_map(
        shard,
        mesh=mesh,
        in_specs=(rows, rows, P(("dp", "fsdp")), P(("fsdp", "ctx"), None), P(), P()),
        out_specs=(rows, P(), P()),
        check_vma=False,
    )
```

```python
import functools
import math

import jax
import jax.numpy as jnp
from jax import lax
from jax.experimental import pallas as pl
from jax.experimental.pallas import tpu as pltpu
from jax.sharding import PartitionSpec as P

MESH = pl.DeviceIdType.MESH
BF16, F32 = jnp.bfloat16, jnp.float32
X, Z = 4, 8
OFFSETS = (0, -1, 1, -2, 2, -3, 3, 4)
SEMS = dict(
    local=6, tok=4, tok2=2, mate=7, zp=7, zm=7, cross=8, pair=8, out=64,
    s1=1, s2=3, s3=7, s4=1, s5=7, s6=1, s7=7, s8=3, s9=1, s10=1,
)
BASE, TOTAL = {}, 0
for _name, _count in SEMS.items():
    BASE[_name] = TOTAL
    TOTAL += _count


def last(a, b):
    return lax.dot_general(a, b, (((1,), (1,)), ((), ())), preferred_element_type=F32)


def wrap(value, size):
    return lax.rem(value + size, size)


def body(
    lengths, inp, cot, frz, adn, aup,
    og, gd_out, gu_out,
    tok, wts, outs, xin, cotv, dn, up, low2,
    part, part16, q16, r1, r2, share, nrm, r4, g8, r5, fin, r6, c7, c8, c9, c10, gd, gu,
    ssem, rsem,
):
    dp, fsdp, ctx = (lax.axis_index(n) for n in ("dp", "fsdp", "ctx"))
    lo, z, c, x, hi = dp, fsdp // 2, lax.rem(fsdp, 2), ctx // 2, lax.rem(ctx, 2)
    rows, width = cot.shape
    half = rows // 2

    def dev(dx=0, dz=0, dc=0, flip_hi=0, flip_lo=0):
        xx, zz = wrap(x + dx, X), wrap(z + dz, Z)
        cc = 1 - c if dc else c
        hh = 1 - hi if flip_hi else hi
        ll = 1 - lo if flip_lo else lo
        return (ll, zz * 2 + cc, xx * 2 + hh)

    peers = [dict(dx=dx, dc=dc) for dx in range(X) for dc in range(2) if dx or dc]
    peers += [dict(dz=dz) for dz in range(1, Z)]
    peers += [dict(dx=dx, flip_hi=1) for dx in range(X)]
    peers += [dict(flip_hi=1, flip_lo=1), dict(flip_lo=1)]

    sent = []

    def send(src, dst, name, i, **to):
        s = BASE[name] + i
        copy = pltpu.make_async_remote_copy(
            src, dst, ssem.at[s], rsem.at[s], device_id=dev(**to), device_id_type=MESH
        )
        copy.start()
        sent.append(copy)

    def got(dst, name, i):
        s = BASE[name] + i
        pltpu.make_async_remote_copy(
            dst, dst, ssem.at[s], rsem.at[s], device_id=dev(dc=1), device_id_type=MESH
        ).wait_recv()

    def local(src, dst, i):
        copy = pltpu.make_async_copy(src, dst, rsem.at[BASE["local"] + i])
        copy.start()
        return copy

    own = x * 2 + c

    def slot(dx, dc=0):
        return wrap(x + dx, X) * 2 + (1 - c if dc else c)

    def wz(d):
        return wrap(z + d, Z)

    cot2, frz2 = cot.reshape(2, half, width), frz.reshape(2, half, width)

    loads = [
        local(aup, up, 0),
        local(cot2, tok.at[own], 1),
        local(adn, dn, 2),
        local(inp, xin, 3),
        local(frz2, wts.at[z, hi], 4),
        local(cot, cotv, 5),
    ]
    barrier = pltpu.get_barrier_semaphore()
    for p in peers:
        pl.semaphore_signal(barrier, inc=1, device_id=dev(**p), device_id_type=MESH)
    pl.semaphore_wait(barrier, len(peers))

    send(cot2.at[0], tok.at[own, 0], "tok", 0, dx=1)
    send(cot2.at[1], tok.at[own, 1], "tok", 3, dx=-1)
    send(frz2.at[lo], wts.at[z, hi, lo], "zp", 0, dz=1)
    send(frz2.at[lo], wts.at[z, hi, lo], "zm", 0, dz=-1)
    send(frz2.at[lo], wts.at[z, hi, lo], "cross", 0, flip_hi=1, flip_lo=1)
    send(cot2.at[1], tok.at[own, 1], "tok", 1, dx=1)
    send(cot2.at[0], tok.at[own, 0], "tok", 2, dx=-1)
    send(frz2.at[1 - lo], wts.at[z, hi, 1 - lo], "zp", 1, dz=1)
    send(frz2.at[1 - lo], wts.at[z, hi, 1 - lo], "zm", 1, dz=-1)
    send(cot2, tok.at[own], "mate", 0, dc=1)

    def partials():
        for i in (0, 5, 2, 3):
            loads[i].wait()
        position = ctx * rows + lax.broadcasted_iota(jnp.int32, (1, rows), 1)
        live = position < lengths[0]
        mine = cotv[...]
        lowered = jnp.where(live, last(up[...], mine), 0.0).astype(BF16)
        proj = jnp.where(live, last(dn[...], xin[...]), 0.0).astype(BF16)
        dcol, ucol = xin.shape[1] // (2 * X), width // (2 * X)
        for i in range(2 * X):
            j, keep = (i % X) * 2 + ((1 - hi) if i < X else hi), i >= X
            a = xin[:, pl.ds(pl.multiple_of(j * dcol, dcol), dcol)]
            pd = 2.0 * jnp.dot(lowered, a, preferred_element_type=F32)
            b = cotv[:, pl.ds(pl.multiple_of(j * ucol, ucol), ucol)]
            pu = 2.0 * jnp.dot(proj, b, preferred_element_type=F32)
            to = part if keep else part16
            to[i % X, :, :dcol] = pd.astype(to.dtype)
            to[i % X, :, dcol:] = pu.astype(to.dtype)
            if i == X - 1:
                send(part16, r1, "s1", 0, flip_hi=1)

    def stage2():
        got(r1, "s1", 0)
        part[...] = part[...] + r1[...].astype(F32)
        q16[...] = part[...].astype(BF16)
        for dx in range(1, X):
            send(q16.at[wrap(x + dx, X)], r2.at[dx - 1], "s2", dx - 1, dx=dx)

    def stage3():
        for dx in range(1, X):
            got(r2.at[dx - 1], "s2", dx - 1)
        total = part[x]
        for i in range(X - 1):
            total = total + r2[i].astype(F32)
        n = total.shape[1] // 2
        share[0] = total[:, :n]
        share[1] = total[:, n:]
        square = jnp.sum(jnp.sum(total * total, axis=1, keepdims=True), axis=0, keepdims=True)
        nrm[ctx] = jnp.broadcast_to(square, nrm.shape[1:])
        for i in range(1, 2 * X):
            send(nrm.at[ctx], nrm.at[ctx], "s3", i - 1, dx=i // 2, flip_hi=i % 2)

    def stage4():
        for i in range(1, 2 * X):
            src = wrap(x - i // 2, X) * 2 + (1 - hi if i % 2 else hi)
            got(nrm.at[src], "s3", i - 1)
        square = nrm[0]
        for i in range(1, 2 * X):
            square = square + nrm[i]
        bound = 10.0 * math.sqrt(dn.shape[0] * (xin.shape[1] + width))
        factor = (bound / jnp.maximum(jnp.sqrt(square), bound))[:1, :1]
        share[...] = share[...] * factor.reshape(1, 1, 1)
        send(share.at[1 - c], r4, "s4", 0, dc=1)

    def stage5():
        got(r4, "s4", 0)
        both = share[c] + r4[...]
        n = g8.shape[2]
        for o in range(Z):
            if o < 6:
                g8[o] = both[(o % 2) * 8 : (o % 2) * 8 + 8, (o // 2) * n : (o // 2 + 1) * n]
            else:
                g8[o] = jnp.zeros(g8.shape[1:], F32)
        for dz in range(1, Z):
            send(g8.at[wz(dz)], r5.at[dz - 1], "s5", dz - 1, dz=dz)

    def stage6():
        total = g8[z]
        for dz in range(1, Z):
            got(r5.at[dz - 1], "s5", dz - 1)
            total = total + r5[dz - 1]
        fin[...] = total
        send(fin, r6, "s6", 0, flip_lo=1)

    def stage7():
        got(r6, "s6", 0)
        c7[z] = (fin[...] + r6[...]) * (1.0 / 32.0)
        for dz in range(1, Z):
            send(c7.at[z], c7.at[z], "s7", dz - 1, dz=dz)

    def stage8():
        for dz in range(1, Z):
            got(c7.at[wz(-dz)], "s7", dz - 1)
        c8[x] = c7[:6]
        for dx in range(1, X):
            send(c7.at[pl.ds(0, 6)], c8.at[x], "s8", dx - 1, dx=dx)

    def stage9():
        for dx in range(1, X):
            got(c8.at[wrap(x - dx, X)], "s8", dx - 1)
        c9[hi] = c8[...]
        send(c8, c9.at[hi], "s9", 0, flip_hi=1, flip_lo=1)

    def stage10():
        got(c9.at[1 - hi], "s9", 0)
        c10[c] = c9[...]
        send(c9, c10.at[c], "s10", 0, dc=1)

    def finish():
        got(c10.at[1 - c], "s10", 0)
        n = g8.shape[2]
        dcol, ucol = xin.shape[1] // (2 * X), width // (2 * X)
        for j in range(2 * X):
            for cc in range(2):
                for o in range(6):
                    r = slice((o % 2) * 8, (o % 2) * 8 + 8)
                    v = c10[cc, j % 2, j // 2, o]
                    at = cc * 3 * n + (o // 2) * n
                    k = max(0, min(n, dcol - at))
                    if k:
                        gd[r, j * dcol + at : j * dcol + at + k] = v[:, :k]
                    if k < n:
                        u = at + k - dcol
                        gu[r, j * ucol + u : j * ucol + u + n - k] = v[:, k:]
        step = xin.shape[1] // 4
        for i in range(4):
            at = pl.ds(i * step, step)
            kept.append(local(gd.at[:, at], gd_out.at[:, at], i))
        kept.append(local(gu, gu_out, 4))

    def weights(k):
        d, which = (k + 1) // 2, (lo if k % 2 else 1 - lo)
        at = wts.at[wz(-d), hi, which]
        got(at, "zp", k - 1)
        if k <= 5:
            send(at, at, "zp", k + 1, dz=1)
        if k % 2:
            send(at, at, "cross", OFFSETS.index(-d if d < 4 else 4), flip_hi=1, flip_lo=1)
        if k == 7:
            which = 1 - lo
        at = wts.at[wz(d), hi, which]
        got(at, "zm", k - 1)
        if k <= 4:
            send(at, at, "zm", k + 1, dz=-1)
        if k == 6:
            send(at, at, "zm", 6, dz=-1)
        if k % 2 and k < 7:
            send(at, at, "cross", OFFSETS.index(d), flip_hi=1, flip_lo=1)

    def across(k):
        at = wts.at[wz(OFFSETS[k - 1]), 1 - hi, 1 - lo]
        got(at, "cross", k - 1)
        send(at, at, "pair", k - 1, flip_lo=1)

    def tokens(k):
        if k == 3:
            moved = ((slot(2), 0, "tok2", 0), (slot(2), 1, "tok2", 1))
        else:
            a, b = (0, 1) if k == 1 else (1, 0)
            moved = ((slot(-1), a, "tok", a), (slot(1), b, "tok", 2 + b))
        for i, (s, part_, name, index) in enumerate(moved):
            at = tok.at[s, part_]
            got(at, name, index)
            if k == 1:
                send(at, at, "tok2", i, dx=1 if i == 0 else -1)
            send(at, at, "mate", 1 + 2 * (k - 1) + i, dc=1)

    kept = []

    def chunk(i, dx, cols):
        shard, xx = wz(OFFSETS[i - 1]), wrap(x + dx, X)
        t = tok[pl.ds(xx * 2, 2)].reshape(2 * rows, width)
        if i == 1:
            lowered = last(t, up[...]).astype(BF16)
            low2[xx] = lowered + lowered
        value = last(t, wts[shard].reshape(2 * rows, width))
        value = value + jnp.dot(low2[xx], dn[:, cols], preferred_element_type=F32)
        outs[i - 1, pl.ds(xx * 2, 2)] = value.astype(BF16).reshape(2, rows, 2 * rows)

    def deliver(i, dx, dc, cols):
        s = BASE["out"] + (i - 1) * 8 + dx * 2 + dc
        return pltpu.make_async_remote_copy(
            outs.at[i - 1, slot(dx, dc)], og.at[:, cols], ssem.at[s], rsem.at[s],
            device_id=dev(dx=dx, dc=dc), device_id_type=MESH,
        )

    def product(i):
        if i == 1:
            loads[1].wait()
            loads[4].wait()
        shard = wz(OFFSETS[i - 1])
        got(wts.at[shard, 1 - hi, lo], "pair", i - 1)
        at = pl.multiple_of(((shard * 2 + c) * 8 + x * 2) * rows, 2 * rows)
        cols = pl.ds(at, 2 * rows)
        if i == 1:
            for k, (d, halves) in enumerate(((-1, (0, 1)), (1, (1, 0)))):
                got(tok.at[slot(d, 1), halves[0]], "mate", 1 + k)
                got(tok.at[slot(d, 1), halves[1]], "mate", 3 + k)
            for dx in (1, 3, 2, 0):
                if dx == 2:
                    got(tok.at[slot(2, 1), 0], "mate", 5)
                    got(tok.at[slot(2, 1), 1], "mate", 6)
                if dx == 0:
                    got(tok.at[slot(0, 1)], "mate", 0)
                chunk(i, dx, cols)
                if dx:
                    for dc in range(2):
                        deliver(i, dx, dc, cols).start()
        else:

            @pl.loop(0, 3)
            def _(t):
                dx = 2 - t + 3 * (t // 2)
                chunk(i, dx, cols)
                for dc in range(2):
                    deliver(i, dx, dc, cols).start()

            chunk(i, 0, cols)
        for dx in range(1, X):
            for dc in range(2):
                sent.append(deliver(i, dx, dc, cols))
        send(outs.at[i - 1, slot(0, 1)], og.at[:, cols], "out", (i - 1) * 8 + 1, dc=1)
        copy = pltpu.make_async_copy(
            outs.at[i - 1, own], og.at[:, cols], rsem.at[BASE["out"] + (i - 1) * 8]
        )
        copy.start()
        kept.append(copy)

    def landed(i):
        shard = wz(OFFSETS[i - 1])
        for dx in range(X):
            for dc in range(2):
                if dx or dc:
                    cc = 1 - c if dc else c
                    at = pl.multiple_of(
                        ((shard * 2 + cc) * 8 + wrap(x - dx, X) * 2) * rows, 2 * rows
                    )
                    got(og.at[:, pl.ds(at, 2 * rows)], "out", (i - 1) * 8 + dx * 2 + dc)

    partials()
    tokens(1)
    weights(1)
    stage2()
    tokens(2)
    across(1)
    weights(2)
    after = {1: stage4, 2: stage5, 3: stage6, 4: stage7, 5: stage8, 7: stage9, 8: stage10}
    for k in range(2, 10):
        if k <= 8:
            across(k)
        if k <= 6:
            weights(k + 1)
        if k == 2:
            tokens(3)
            stage3()
        product(k - 1)
        if k - 1 in after:
            after[k - 1]()
    finish()
    for i in range(1, 9):
        landed(i)
    for copy in kept:
        copy.wait()
    for copy in sent:
        copy.wait_send()


def fused(lengths, inp, cot, frz, adn, aup):
    rows, width = cot.shape
    rank, features = adn.shape
    share = (features + width) // (2 * X)
    n = share // 6
    scratch = [
        pltpu.VMEM((2 * X, 2, rows // 2, width), BF16),
        pltpu.VMEM((Z, 2, 2, rows // 2, width), BF16),
        pltpu.VMEM((Z, 2 * X, rows, 2 * rows), BF16),
        pltpu.VMEM((rows, features), BF16),
        pltpu.VMEM((rows, width), BF16),
        pltpu.VMEM((rank, features), BF16),
        pltpu.VMEM((rank, width), BF16),
        pltpu.VMEM((4, 2 * rows, rank), BF16),
        pltpu.VMEM((X, rank, share), F32),
        pltpu.VMEM((X, rank, share), BF16),
        pltpu.VMEM((X, rank, share), BF16),
        pltpu.VMEM((X, rank, share), BF16),
        pltpu.VMEM((X - 1, rank, share), BF16),
        pltpu.VMEM((2, rank, share // 2), F32),
        pltpu.VMEM((2 * X, 8, 128), F32),
        pltpu.VMEM((rank, share // 2), F32),
        pltpu.VMEM((Z, 8, n), F32),
        pltpu.VMEM((Z - 1, 8, n), F32),
        pltpu.VMEM((8, n), F32),
        pltpu.VMEM((8, n), F32),
        pltpu.VMEM((Z, 8, n), F32),
        pltpu.VMEM((X, 6, 8, n), F32),
        pltpu.VMEM((2, X, 6, 8, n), F32),
        pltpu.VMEM((2, 2, X, 6, 8, n), F32),
        pltpu.VMEM((rank, features), F32),
        pltpu.VMEM((rank, width), F32),
        pltpu.SemaphoreType.DMA((TOTAL,)),
        pltpu.SemaphoreType.DMA((TOTAL,)),
    ]
    anywhere = pl.BlockSpec(memory_space=pl.ANY)
    hbm = pl.BlockSpec(memory_space=pltpu.HBM)
    return pl.pallas_call(
        body,
        out_shape=(
            jax.ShapeDtypeStruct((rows, features), BF16),
            jax.ShapeDtypeStruct((rank, features), F32),
            jax.ShapeDtypeStruct((rank, width), F32),
        ),
        in_specs=[pl.BlockSpec(memory_space=pltpu.SMEM)] + [hbm] * 5,
        out_specs=(anywhere, anywhere, anywhere),
        scratch_shapes=scratch,
        compiler_params=pltpu.CompilerParams(
            collective_id=0, has_side_effects=True, vmem_limit_bytes=44 << 20
        ),
    )(lengths, *(pltpu.with_memory_space_constraint(a, pltpu.HBM) for a in (inp, cot, frz, adn, aup)))


def shard(inputs, cotangent, lengths, frozen, adapter_down, adapter_up):
    _, rows, features = inputs.shape
    raw, grad_down, grad_up = fused(
        lengths, inputs[0], cotangent[0], frozen, adapter_down, adapter_up
    )
    position = lax.axis_index("ctx") * rows + jnp.arange(rows, dtype=jnp.int32)
    live = position[:, None] < lengths
    input_grads = jnp.where(live, raw, jnp.zeros((), BF16))
    return input_grads[None], grad_down, grad_up


def solution(mesh):
    rows = P(("dp", "fsdp"), "ctx", None)
    return jax.shard_map(
        shard,
        mesh=mesh,
        in_specs=(rows, rows, P(("dp", "fsdp")), P(("fsdp", "ctx"), None), P(), P()),
        out_specs=(rows, P(), P()),
        check_vma=False,
    )
```

```python
import functools
import math

import jax
import jax.numpy as jnp
from jax import lax
from jax.experimental import pallas as pl
from jax.experimental.pallas import tpu as pltpu
from jax.sharding import PartitionSpec as P

MESH = pl.DeviceIdType.MESH
BF16, F32 = jnp.bfloat16, jnp.float32
X, Z = 4, 8
OFFSETS = (0, -1, 1, -2, 2, -3, 3, 4)
SEMS = dict(
    local=6, tok=4, tok2=2, mate=7, zp=7, zm=7, cross=8, pair=8, out=8, outs=1,
    s1=1, s2=3, s3=7, s4=1, s5=7, s6=1, s7=7, s8=3, s9=1, s10=1,
)
BASE, TOTAL = {}, 0
for _name, _count in SEMS.items():
    BASE[_name] = TOTAL
    TOTAL += _count


def last(a, b):
    return lax.dot_general(a, b, (((1,), (1,)), ((), ())), preferred_element_type=F32)


def wrap(value, size):
    return lax.rem(value + size, size)


def body(
    lengths, inp, cot, frz, adn, aup,
    og, gd_out, gu_out,
    tok, wts, outs, xin, cotv, dn, up, low2,
    part, part16, q16, r1, r2, share, nrm, r4, r6, g8, r5, c7, c8, c9, c10, gd, gu,
    ssem, rsem,
):
    dp, fsdp, ctx = (lax.axis_index(n) for n in ("dp", "fsdp", "ctx"))
    lo, z, c, x, hi = dp, fsdp // 2, lax.rem(fsdp, 2), ctx // 2, lax.rem(ctx, 2)
    rows, width = cot.shape
    half = rows // 2

    def dev(dx=0, dz=0, dc=0, flip_hi=0, flip_lo=0):
        xx, zz = wrap(x + dx, X), wrap(z + dz, Z)
        cc = 1 - c if dc else c
        hh = 1 - hi if flip_hi else hi
        ll = 1 - lo if flip_lo else lo
        return (ll, zz * 2 + cc, xx * 2 + hh)

    peers = [dict(dx=dx, dc=dc) for dx in range(X) for dc in range(2) if dx or dc]
    peers += [dict(dz=dz) for dz in range(1, Z)]
    peers += [dict(dx=dx, flip_hi=1) for dx in range(X)]
    peers += [dict(flip_hi=1, flip_lo=1), dict(flip_lo=1)]

    sent = []

    def send(src, dst, name, i, **to):
        s = BASE[name] + i
        copy = pltpu.make_async_remote_copy(
            src, dst, ssem.at[s], rsem.at[s], device_id=dev(**to), device_id_type=MESH
        )
        copy.start()
        sent.append(copy)

    def got(dst, name, i):
        s = BASE[name] + i
        pltpu.make_async_remote_copy(
            dst, dst, ssem.at[s], rsem.at[s], device_id=dev(dc=1), device_id_type=MESH
        ).wait_recv()

    def local(src, dst, i):
        copy = pltpu.make_async_copy(src, dst, rsem.at[BASE["local"] + i])
        copy.start()
        return copy

    own = x * 2 + c

    def slot(dx, dc=0):
        return wrap(x + dx, X) * 2 + (1 - c if dc else c)

    def wz(d):
        return wrap(z + d, Z)

    cot2, frz2 = cot.reshape(2, half, width), frz.reshape(2, half, width)

    loads = [
        local(aup, up, 0),
        local(cot2, tok.at[own], 1),
        local(adn, dn, 2),
        local(inp, xin, 3),
        local(frz2, wts.at[z, hi], 4),
        local(cot, cotv, 5),
    ]
    barrier = pltpu.get_barrier_semaphore()
    for p in peers:
        pl.semaphore_signal(barrier, inc=1, device_id=dev(**p), device_id_type=MESH)
    pl.semaphore_wait(barrier, len(peers))

    send(cot2.at[0], tok.at[own, 0], "tok", 0, dx=1)
    send(cot2.at[1], tok.at[own, 1], "tok", 3, dx=-1)
    send(frz2.at[lo], wts.at[z, hi, lo], "zp", 0, dz=1)
    send(frz2.at[lo], wts.at[z, hi, lo], "zm", 0, dz=-1)
    send(frz2.at[lo], wts.at[z, hi, lo], "cross", 0, flip_hi=1, flip_lo=1)
    send(cot2.at[1], tok.at[own, 1], "tok", 1, dx=1)
    send(cot2.at[0], tok.at[own, 0], "tok", 2, dx=-1)
    send(frz2.at[1 - lo], wts.at[z, hi, 1 - lo], "zp", 1, dz=1)
    send(frz2.at[1 - lo], wts.at[z, hi, 1 - lo], "zm", 1, dz=-1)
    send(cot2, tok.at[own], "mate", 0, dc=1)

    def partials():
        for i in (0, 5, 2, 3):
            loads[i].wait()
        position = ctx * rows + lax.broadcasted_iota(jnp.int32, (1, rows), 1)
        live = position < lengths[0]
        mine = cotv[...]
        lowered = jnp.where(live, last(up[...], mine), 0.0).astype(BF16)
        proj = jnp.where(live, last(dn[...], xin[...]), 0.0).astype(BF16)
        dcol, ucol = xin.shape[1] // (2 * X), width // (2 * X)
        for i in range(2 * X):
            j, keep = (i % X) * 2 + ((1 - hi) if i < X else hi), i >= X
            a = xin[:, pl.ds(pl.multiple_of(j * dcol, dcol), dcol)]
            pd = 2.0 * jnp.dot(lowered, a, preferred_element_type=F32)
            b = cotv[:, pl.ds(pl.multiple_of(j * ucol, ucol), ucol)]
            pu = 2.0 * jnp.dot(proj, b, preferred_element_type=F32)
            to = part if keep else part16
            to[i % X, :, :dcol] = pd.astype(to.dtype)
            to[i % X, :, dcol:] = pu.astype(to.dtype)
            if i == X - 1:
                send(part16, r1, "s1", 0, flip_hi=1)

    def stage2():
        got(r1, "s1", 0)
        part[...] = part[...] + r1[...].astype(F32)
        q16[...] = part[...].astype(BF16)
        for dx in range(1, X):
            send(q16.at[wrap(x + dx, X)], r2.at[dx - 1], "s2", dx - 1, dx=dx)

    def stage3():
        for dx in range(1, X):
            got(r2.at[dx - 1], "s2", dx - 1)
        total = part[x]
        for i in range(X - 1):
            total = total + r2[i].astype(F32)
        n = total.shape[1] // 2
        share[0] = total[:, :n]
        share[1] = total[:, n:]
        square = jnp.sum(jnp.sum(total * total, axis=1, keepdims=True), axis=0, keepdims=True)
        nrm[ctx] = jnp.broadcast_to(square, nrm.shape[1:])
        for i in range(1, 2 * X):
            send(nrm.at[ctx], nrm.at[ctx], "s3", i - 1, dx=i // 2, flip_hi=i % 2)

    def stage4():
        for i in range(1, 2 * X):
            src = wrap(x - i // 2, X) * 2 + (1 - hi if i % 2 else hi)
            got(nrm.at[src], "s3", i - 1)
        square = nrm[0]
        for i in range(1, 2 * X):
            square = square + nrm[i]
        bound = 10.0 * math.sqrt(dn.shape[0] * (xin.shape[1] + width))
        factor = (bound / jnp.maximum(jnp.sqrt(square), bound))[:1, :1]
        share[...] = share[...] * factor.reshape(1, 1, 1)
        send(share.at[1 - c], r4, "s4", 0, dc=1)

    def stage5():
        got(r4, "s4", 0)
        share[c] = share[c] + r4[...]
        send(share.at[c], r6, "s6", 0, flip_lo=1)

    def stage6():
        got(r6, "s6", 0)
        both = share[c] + r6[...]
        n = g8.shape[2]
        for o in range(Z):
            if o < 6:
                g8[o] = both[(o % 2) * 8 : (o % 2) * 8 + 8, (o // 2) * n : (o // 2 + 1) * n]
            else:
                g8[o] = jnp.zeros(g8.shape[1:], F32)
        for dz in range(1, Z):
            send(g8.at[wz(dz)], r5.at[dz - 1], "s5", dz - 1, dz=dz)

    def stage7():
        total = g8[z]
        for dz in range(1, Z):
            got(r5.at[dz - 1], "s5", dz - 1)
            total = total + r5[dz - 1]
        c7[z] = total * (1.0 / 32.0)
        for dz in range(1, Z):
            send(c7.at[z], c7.at[z], "s7", dz - 1, dz=dz)

    def stage8():
        for dz in range(1, Z):
            got(c7.at[wz(-dz)], "s7", dz - 1)
        c8[x] = c7[:6]
        for dx in range(1, X):
            send(c7.at[pl.ds(0, 6)], c8.at[x], "s8", dx - 1, dx=dx)

    def stage9():
        for dx in range(1, X):
            got(c8.at[wrap(x - dx, X)], "s8", dx - 1)
        c9[hi] = c8[...]
        send(c8, c9.at[hi], "s9", 0, flip_hi=1, flip_lo=1)

    def stage10():
        got(c9.at[1 - hi], "s9", 0)
        c10[c] = c9[...]
        send(c9, c10.at[c], "s10", 0, dc=1)

    def finish():
        got(c10.at[1 - c], "s10", 0)
        n = g8.shape[2]
        dcol, ucol = xin.shape[1] // (2 * X), width // (2 * X)
        for j in range(2 * X):
            for cc in range(2):
                for o in range(6):
                    r = slice((o % 2) * 8, (o % 2) * 8 + 8)
                    v = c10[cc, j % 2, j // 2, o]
                    at = cc * 3 * n + (o // 2) * n
                    k = max(0, min(n, dcol - at))
                    if k:
                        gd[r, j * dcol + at : j * dcol + at + k] = v[:, :k]
                    if k < n:
                        u = at + k - dcol
                        gu[r, j * ucol + u : j * ucol + u + n - k] = v[:, k:]
        step = xin.shape[1] // 4
        for i in range(4):
            at = pl.ds(i * step, step)
            kept.append(local(gd.at[:, at], gd_out.at[:, at], i))
        kept.append(local(gu, gu_out, 4))

    def weights(k):
        d, which = (k + 1) // 2, (lo if k % 2 else 1 - lo)
        at = wts.at[wz(-d), hi, which]
        got(at, "zp", k - 1)
        if k <= 5:
            send(at, at, "zp", k + 1, dz=1)
        if k % 2:
            send(at, at, "cross", OFFSETS.index(-d if d < 4 else 4), flip_hi=1, flip_lo=1)
        if k == 7:
            which = 1 - lo
        at = wts.at[wz(d), hi, which]
        got(at, "zm", k - 1)
        if k <= 4:
            send(at, at, "zm", k + 1, dz=-1)
        if k == 6:
            send(at, at, "zm", 6, dz=-1)
        if k % 2 and k < 7:
            send(at, at, "cross", OFFSETS.index(d), flip_hi=1, flip_lo=1)

    def across(k):
        at = wts.at[wz(OFFSETS[k - 1]), 1 - hi, 1 - lo]
        got(at, "cross", k - 1)
        send(at, at, "pair", k - 1, flip_lo=1)

    def tokens(k):
        if k == 3:
            moved = ((slot(2), 0, "tok2", 0), (slot(2), 1, "tok2", 1))
        else:
            a, b = (0, 1) if k == 1 else (1, 0)
            moved = ((slot(-1), a, "tok", a), (slot(1), b, "tok", 2 + b))
        for i, (s, part_, name, index) in enumerate(moved):
            at = tok.at[s, part_]
            got(at, name, index)
            send(at, at, "mate", 1 + 2 * (k - 1) + i, dc=1)
            if k == 1:
                send(at, at, "tok2", i, dx=1 if i == 0 else -1)

    kept = []

    def lower(dx):
        if dx == 0:
            loads[1].wait()
            got(tok.at[slot(0, 1)], "mate", 0)
        elif dx == 2:
            got(tok.at[slot(2, 1), 0], "mate", 5)
            got(tok.at[slot(2, 1), 1], "mate", 6)
        else:
            k = 0 if dx == 3 else 1
            got(tok.at[slot(dx, 1), k], "mate", 1 + k)
            got(tok.at[slot(dx, 1), 1 - k], "mate", 3 + k)
        xx = wrap(x + dx, X)
        t = tok[pl.ds(xx * 2, 2)].reshape(2 * rows, width)
        lowered = last(t, up[...]).astype(BF16)
        low2[xx] = lowered + lowered

    def chunk(i, dx, cols):
        shard, xx = wz(OFFSETS[i - 1]), wrap(x + dx, X)
        t = tok[pl.ds(xx * 2, 2)].reshape(2 * rows, width)
        value = last(t, wts[shard].reshape(2 * rows, width))
        value = value + jnp.dot(low2[xx], dn[:, cols], preferred_element_type=F32)
        outs[i - 1, pl.ds(xx * 2, 2)] = value.astype(BF16).reshape(2, rows, 2 * rows)

    def deliver(i, dx, dc, cols):
        s = BASE["outs"]
        return pltpu.make_async_remote_copy(
            outs.at[i - 1, slot(dx, dc)], og.at[:, cols], ssem.at[s], rsem.at[s],
            device_id=dev(dx=dx, dc=dc), device_id_type=MESH,
        )

    def product(i):
        if i == 1:
            loads[4].wait()
        shard = wz(OFFSETS[i - 1])
        got(wts.at[shard, 1 - hi, lo], "pair", i - 1)
        at = pl.multiple_of(((shard * 2 + c) * 8 + x * 2) * rows, 2 * rows)
        cols = pl.ds(at, 2 * rows)
        if i == 1:
            for dx in (1, 3, 2, 0):
                if dx == 2:
                    lower(2)
                chunk(i, dx, cols)
                if dx:
                    for dc in range(2):
                        deliver(i, dx, dc, cols).start()
        else:

            @pl.loop(0, 3)
            def _(t):
                dx = 2 - t + 3 * (t // 2)
                chunk(i, dx, cols)
                for dc in range(2):
                    deliver(i, dx, dc, cols).start()

            chunk(i, 0, cols)
        deliver(i, 0, 1, cols).start()
        copy = pltpu.make_async_copy(
            outs.at[i - 1, own], og.at[:, cols], rsem.at[BASE["out"] + i - 1]
        )
        copy.start()
        kept.append(copy)

    partials()
    tokens(1)
    weights(1)
    stage2()
    tokens(2)
    across(1)
    weights(2)
    lower(0)
    lower(1)
    lower(3)
    across(2)
    weights(3)
    tokens(3)
    stage3()
    product(1)
    across(3)
    weights(4)
    stage4()
    product(2)
    stage5()
    weights(5)
    across(4)
    product(3)
    stage6()
    weights(6)
    across(5)
    product(4)
    stage7()
    weights(7)
    across(6)
    product(5)
    stage8()
    across(7)
    product(6)
    across(8)
    product(7)
    stage9()
    product(8)
    stage10()
    finish()
    for copy in kept:
        copy.wait()
    s = BASE["outs"]
    moved = outs.at[pl.ds(0, 7)]
    every = pltpu.make_async_remote_copy(
        moved, moved, ssem.at[s], rsem.at[s], device_id=dev(dc=1), device_id_type=MESH
    )
    every.wait()
    for copy in sent:
        copy.wait_send()


def fused(lengths, inp, cot, frz, adn, aup):
    rows, width = cot.shape
    rank, features = adn.shape
    share = (features + width) // (2 * X)
    n = share // 6
    scratch = [
        pltpu.VMEM((2 * X, 2, rows // 2, width), BF16),
        pltpu.VMEM((Z, 2, 2, rows // 2, width), BF16),
        pltpu.VMEM((Z, 2 * X, rows, 2 * rows), BF16),
        pltpu.VMEM((rows, features), BF16),
        pltpu.VMEM((rows, width), BF16),
        pltpu.VMEM((rank, features), BF16),
        pltpu.VMEM((rank, width), BF16),
        pltpu.VMEM((4, 2 * rows, rank), BF16),
        pltpu.VMEM((X, rank, share), F32),
        pltpu.VMEM((X, rank, share), BF16),
        pltpu.VMEM((X, rank, share), BF16),
        pltpu.VMEM((X, rank, share), BF16),
        pltpu.VMEM((X - 1, rank, share), BF16),
        pltpu.VMEM((2, rank, share // 2), F32),
        pltpu.VMEM((2 * X, 8, 128), F32),
        pltpu.VMEM((rank, share // 2), F32),
        pltpu.VMEM((rank, share // 2), F32),
        pltpu.VMEM((Z, 8, n), F32),
        pltpu.VMEM((Z - 1, 8, n), F32),
        pltpu.VMEM((Z, 8, n), F32),
        pltpu.VMEM((X, 6, 8, n), F32),
        pltpu.VMEM((2, X, 6, 8, n), F32),
        pltpu.VMEM((2, 2, X, 6, 8, n), F32),
        pltpu.VMEM((rank, features), F32),
        pltpu.VMEM((rank, width), F32),
        pltpu.SemaphoreType.DMA((TOTAL,)),
        pltpu.SemaphoreType.DMA((TOTAL,)),
    ]
    anywhere = pl.BlockSpec(memory_space=pl.ANY)
    hbm = pl.BlockSpec(memory_space=pltpu.HBM)
    return pl.pallas_call(
        body,
        out_shape=(
            jax.ShapeDtypeStruct((rows, features), BF16),
            jax.ShapeDtypeStruct((rank, features), F32),
            jax.ShapeDtypeStruct((rank, width), F32),
        ),
        in_specs=[pl.BlockSpec(memory_space=pltpu.SMEM)] + [hbm] * 5,
        out_specs=(anywhere, anywhere, anywhere),
        scratch_shapes=scratch,
        compiler_params=pltpu.CompilerParams(
            collective_id=0, has_side_effects=True, vmem_limit_bytes=44 << 20
        ),
    )(lengths, *(pltpu.with_memory_space_constraint(a, pltpu.HBM) for a in (inp, cot, frz, adn, aup)))


def shard(inputs, cotangent, lengths, frozen, adapter_down, adapter_up):
    _, rows, features = inputs.shape
    raw, grad_down, grad_up = fused(
        lengths, inputs[0], cotangent[0], frozen, adapter_down, adapter_up
    )
    position = lax.axis_index("ctx") * rows + jnp.arange(rows, dtype=jnp.int32)
    live = position[:, None] < lengths
    input_grads = jnp.where(live, raw, jnp.zeros((), BF16))
    return input_grads[None], grad_down, grad_up


def solution(mesh):
    rows = P(("dp", "fsdp"), "ctx", None)
    return jax.shard_map(
        shard,
        mesh=mesh,
        in_specs=(rows, rows, P(("dp", "fsdp")), P(("fsdp", "ctx"), None), P(), P()),
        out_specs=(rows, P(), P()),
        check_vma=False,
    )
```

```python
import functools
import math

import jax
import jax.numpy as jnp
from jax import lax
from jax.experimental import pallas as pl
from jax.experimental.pallas import tpu as pltpu
from jax.sharding import PartitionSpec as P

MESH = pl.DeviceIdType.MESH
BF16, F32 = jnp.bfloat16, jnp.float32
X, Z = 4, 8
OFFSETS = (0, -1, 1, -2, 2, -3, 3, 4)
SEMS = dict(
    local=6, tok=4, tok2=2, mate=7, zp=7, zm=7, cross=8, pair=8, out=1, outs=1,
    s1=1, s2=1, s3=1, s4=1, s5=1, s6=1, s7=1, s8=1, s9=1, s10=1,
)
BASE, TOTAL = {}, 0
for _name, _count in SEMS.items():
    BASE[_name] = TOTAL
    TOTAL += _count
GROUP = dict(tok=0, tok2=0, mate=0, zp=1, zm=1, cross=1, pair=1, outs=2)
GROUP.update({f"s{i}": i + 2 for i in range(1, 11)})


def last(a, b):
    return lax.dot_general(a, b, (((1,), (1,)), ((), ())), preferred_element_type=F32)


def wrap(value, size):
    return lax.rem(value + size, size)


def body(
    lengths, inp, cot, frz, adn, aup,
    og, gd_out, gu_out,
    tok, wts, outs, xin, cotv, dn, up, low2,
    part, part16, q16, r1, r2, share, nrm, r4, r6, g8, r5, c7, c8, c9, c10, gd, gu,
    ssem, rsem,
):
    dp, fsdp, ctx = (lax.axis_index(n) for n in ("dp", "fsdp", "ctx"))
    lo, z, c, x, hi = dp, fsdp // 2, lax.rem(fsdp, 2), ctx // 2, lax.rem(ctx, 2)
    rows, width = cot.shape
    half = rows // 2

    def dev(dx=0, dz=0, dc=0, flip_hi=0, flip_lo=0):
        xx, zz = wrap(x + dx, X), wrap(z + dz, Z)
        cc = 1 - c if dc else c
        hh = 1 - hi if flip_hi else hi
        ll = 1 - lo if flip_lo else lo
        return (ll, zz * 2 + cc, xx * 2 + hh)

    peers = [dict(dx=dx, dc=dc) for dx in range(X) for dc in range(2) if dx or dc]
    peers += [dict(dz=dz) for dz in range(1, Z)]
    peers += [dict(dx=dx, flip_hi=1) for dx in range(X)]
    peers += [dict(flip_hi=1, flip_lo=1), dict(flip_lo=1)]

    def send(src, dst, name, i, **to):
        r = BASE[name] + min(i, SEMS[name] - 1)
        pltpu.make_async_remote_copy(
            src, dst, ssem.at[GROUP[name]], rsem.at[r], device_id=dev(**to), device_id_type=MESH
        ).start()

    def got(dst, name, i=0):
        pltpu.make_async_remote_copy(
            dst, dst, ssem.at[GROUP[name]], rsem.at[BASE[name] + i],
            device_id=dev(dc=1), device_id_type=MESH,
        ).wait_recv()

    def left(src, name):
        pltpu.make_async_remote_copy(
            src, src, ssem.at[GROUP[name]], rsem.at[BASE[name]],
            device_id=dev(dc=1), device_id_type=MESH,
        ).wait_send()

    def local(src, dst, i):
        copy = pltpu.make_async_copy(src, dst, rsem.at[BASE["local"] + i])
        copy.start()
        return copy

    own = x * 2 + c

    def slot(dx, dc=0):
        return wrap(x + dx, X) * 2 + (1 - c if dc else c)

    def wz(d):
        return wrap(z + d, Z)

    cot2, frz2 = cot.reshape(2, half, width), frz.reshape(2, half, width)

    loads = [
        local(aup, up, 0),
        local(cot2, tok.at[own], 1),
        local(adn, dn, 2),
        local(inp, xin, 3),
        local(frz2, wts.at[z, hi], 4),
        local(cot, cotv, 5),
    ]
    barrier = pltpu.get_barrier_semaphore()
    for p in peers:
        pl.semaphore_signal(barrier, inc=1, device_id=dev(**p), device_id_type=MESH)
    pl.semaphore_wait(barrier, len(peers))

    send(cot2.at[0], tok.at[own, 0], "tok", 0, dx=1)
    send(cot2.at[1], tok.at[own, 1], "tok", 3, dx=-1)
    send(frz2.at[lo], wts.at[z, hi, lo], "zp", 0, dz=1)
    send(frz2.at[lo], wts.at[z, hi, lo], "zm", 0, dz=-1)
    send(frz2.at[lo], wts.at[z, hi, lo], "cross", 0, flip_hi=1, flip_lo=1)
    send(cot2.at[1], tok.at[own, 1], "tok", 1, dx=1)
    send(cot2.at[0], tok.at[own, 0], "tok", 2, dx=-1)
    send(frz2.at[1 - lo], wts.at[z, hi, 1 - lo], "zp", 1, dz=1)
    send(frz2.at[1 - lo], wts.at[z, hi, 1 - lo], "zm", 1, dz=-1)
    send(cot2, tok.at[own], "mate", 0, dc=1)

    def partials():
        for i in (0, 5, 2, 3):
            loads[i].wait()
        position = ctx * rows + lax.broadcasted_iota(jnp.int32, (1, rows), 1)
        live = position < lengths[0]
        mine = cotv[...]
        lowered = jnp.where(live, last(up[...], mine), 0.0).astype(BF16)
        proj = jnp.where(live, last(dn[...], xin[...]), 0.0).astype(BF16)
        dcol, ucol = xin.shape[1] // (2 * X), width // (2 * X)
        for i in range(2 * X):
            j, keep = (i % X) * 2 + ((1 - hi) if i < X else hi), i >= X
            a = xin[:, pl.ds(pl.multiple_of(j * dcol, dcol), dcol)]
            pd = 2.0 * jnp.dot(lowered, a, preferred_element_type=F32)
            b = cotv[:, pl.ds(pl.multiple_of(j * ucol, ucol), ucol)]
            pu = 2.0 * jnp.dot(proj, b, preferred_element_type=F32)
            to = part if keep else part16
            to[i % X, :, :dcol] = pd.astype(to.dtype)
            to[i % X, :, dcol:] = pu.astype(to.dtype)
            if i == X - 1:
                send(part16, r1, "s1", 0, flip_hi=1)

    def stage2():
        got(r1, "s1", 0)
        part[...] = part[...] + r1[...].astype(F32)
        q16[...] = part[...].astype(BF16)
        for dx in range(1, X):
            send(q16.at[wrap(x + dx, X)], r2.at[dx - 1], "s2", dx - 1, dx=dx)

    def stage3():
        got(r2, "s2")
        total = part[x]
        for i in range(X - 1):
            total = total + r2[i].astype(F32)
        n = total.shape[1] // 2
        share[0] = total[:, :n]
        share[1] = total[:, n:]
        square = jnp.sum(jnp.sum(total * total, axis=1, keepdims=True), axis=0, keepdims=True)
        nrm[ctx] = jnp.broadcast_to(square, nrm.shape[1:])
        for i in range(1, 2 * X):
            send(nrm.at[ctx], nrm.at[ctx], "s3", i - 1, dx=i // 2, flip_hi=i % 2)

    def stage4():
        got(nrm.at[pl.ds(0, 7)], "s3")
        square = nrm[0]
        for i in range(1, 2 * X):
            square = square + nrm[i]
        bound = 10.0 * math.sqrt(dn.shape[0] * (xin.shape[1] + width))
        factor = (bound / jnp.maximum(jnp.sqrt(square), bound))[:1, :1]
        share[...] = share[...] * factor.reshape(1, 1, 1)
        send(share.at[1 - c], r4, "s4", 0, dc=1)

    def stage5():
        got(r4, "s4", 0)
        share[c] = share[c] + r4[...]
        send(share.at[c], r6, "s6", 0, flip_lo=1)

    def stage6():
        got(r6, "s6", 0)
        both = share[c] + r6[...]
        n = g8.shape[2]
        for o in range(Z):
            if o < 6:
                g8[o] = both[(o % 2) * 8 : (o % 2) * 8 + 8, (o // 2) * n : (o // 2 + 1) * n]
            else:
                g8[o] = jnp.zeros(g8.shape[1:], F32)
        for dz in range(1, Z):
            send(g8.at[wz(dz)], r5.at[dz - 1], "s5", dz - 1, dz=dz)

    def stage7():
        got(r5, "s5")
        total = g8[z]
        for dz in range(1, Z):
            total = total + r5[dz - 1]
        c7[z] = total * (1.0 / 32.0)
        for dz in range(1, Z):
            send(c7.at[z], c7.at[z], "s7", dz - 1, dz=dz)

    def stage8():
        got(c7.at[pl.ds(0, 7)], "s7")
        c8[x] = c7[:6]
        for dx in range(1, X):
            send(c7.at[pl.ds(0, 6)], c8.at[x], "s8", dx - 1, dx=dx)

    def stage9():
        got(c8.at[pl.ds(0, 3)], "s8")
        c9[hi] = c8[...]
        send(c8, c9.at[hi], "s9", 0, flip_hi=1, flip_lo=1)

    def stage10():
        got(c9.at[1 - hi], "s9", 0)
        c10[c] = c9[...]
        send(c9, c10.at[c], "s10", 0, dc=1)

    def finish():
        got(c10.at[1 - c], "s10", 0)
        n = g8.shape[2]
        dcol, ucol = xin.shape[1] // (2 * X), width // (2 * X)
        for j in range(2 * X):
            for cc in range(2):
                for o in range(6):
                    r = slice((o % 2) * 8, (o % 2) * 8 + 8)
                    v = c10[cc, j % 2, j // 2, o]
                    at = cc * 3 * n + (o // 2) * n
                    k = max(0, min(n, dcol - at))
                    if k:
                        gd[r, j * dcol + at : j * dcol + at + k] = v[:, :k]
                    if k < n:
                        u = at + k - dcol
                        gu[r, j * ucol + u : j * ucol + u + n - k] = v[:, k:]
        step = xin.shape[1] // 4
        for i in range(4):
            at = pl.ds(i * step, step)
            kept.append(local(gd.at[:, at], gd_out.at[:, at], i))
        kept.append(local(gu, gu_out, 4))

    def weights(k):
        d, which = (k + 1) // 2, (lo if k % 2 else 1 - lo)
        at = wts.at[wz(-d), hi, which]
        got(at, "zp", k - 1)
        if k <= 5:
            send(at, at, "zp", k + 1, dz=1)
        if k % 2:
            send(at, at, "cross", OFFSETS.index(-d if d < 4 else 4), flip_hi=1, flip_lo=1)
        if k == 7:
            which = 1 - lo
        at = wts.at[wz(d), hi, which]
        got(at, "zm", k - 1)
        if k <= 4:
            send(at, at, "zm", k + 1, dz=-1)
        if k == 6:
            send(at, at, "zm", 6, dz=-1)
        if k % 2 and k < 7:
            send(at, at, "cross", OFFSETS.index(d), flip_hi=1, flip_lo=1)

    def across(k):
        at = wts.at[wz(OFFSETS[k - 1]), 1 - hi, 1 - lo]
        got(at, "cross", k - 1)
        send(at, at, "pair", k - 1, flip_lo=1)

    def tokens(k):
        if k == 3:
            moved = ((slot(2), 0, "tok2", 0), (slot(2), 1, "tok2", 1))
        else:
            a, b = (0, 1) if k == 1 else (1, 0)
            moved = ((slot(-1), a, "tok", a), (slot(1), b, "tok", 2 + b))
        for i, (s, part_, name, index) in enumerate(moved):
            at = tok.at[s, part_]
            got(at, name, index)
            send(at, at, "mate", 1 + 2 * (k - 1) + i, dc=1)
            if k == 1:
                send(at, at, "tok2", i, dx=1 if i == 0 else -1)

    kept = []

    def lower(dx):
        if dx == 0:
            loads[1].wait()
            got(tok.at[slot(0, 1)], "mate", 0)
        elif dx == 2:
            got(tok.at[slot(2, 1), 0], "mate", 5)
            got(tok.at[slot(2, 1), 1], "mate", 6)
        else:
            k = 0 if dx == 3 else 1
            got(tok.at[slot(dx, 1), k], "mate", 1 + k)
            got(tok.at[slot(dx, 1), 1 - k], "mate", 3 + k)
        xx = wrap(x + dx, X)
        t = tok[pl.ds(xx * 2, 2)].reshape(2 * rows, width)
        lowered = last(t, up[...]).astype(BF16)
        low2[xx] = lowered + lowered

    def chunk(i, dx, cols):
        shard, xx = wz(OFFSETS[i - 1]), wrap(x + dx, X)
        t = tok[pl.ds(xx * 2, 2)].reshape(2 * rows, width)
        value = last(t, wts[shard].reshape(2 * rows, width))
        value = value + jnp.dot(low2[xx], dn[:, cols], preferred_element_type=F32)
        outs[i - 1, pl.ds(xx * 2, 2)] = value.astype(BF16).reshape(2, rows, 2 * rows)

    def deliver(i, dx, dc, cols):
        return pltpu.make_async_remote_copy(
            outs.at[i - 1, slot(dx, dc)], og.at[:, cols],
            ssem.at[GROUP["outs"]], rsem.at[BASE["outs"]],
            device_id=dev(dx=dx, dc=dc), device_id_type=MESH,
        )

    def product(i):
        if i == 1:
            loads[4].wait()
        shard = wz(OFFSETS[i - 1])
        got(wts.at[shard, 1 - hi, lo], "pair", i - 1)
        at = pl.multiple_of(((shard * 2 + c) * 8 + x * 2) * rows, 2 * rows)
        cols = pl.ds(at, 2 * rows)
        if i == 1:
            for dx in (1, 3, 2, 0):
                if dx == 2:
                    lower(2)
                chunk(i, dx, cols)
                if dx:
                    for dc in range(2):
                        deliver(i, dx, dc, cols).start()
        else:

            @pl.loop(0, 3)
            def _(t):
                dx = 2 - t + 3 * (t // 2)
                chunk(i, dx, cols)
                for dc in range(2):
                    deliver(i, dx, dc, cols).start()

            chunk(i, 0, cols)
        deliver(i, 0, 1, cols).start()
        pltpu.make_async_copy(outs.at[i - 1, own], og.at[:, cols], rsem.at[BASE["out"]]).start()

    partials()
    tokens(1)
    weights(1)
    stage2()
    tokens(2)
    across(1)
    weights(2)
    lower(0)
    lower(1)
    lower(3)
    across(2)
    weights(3)
    tokens(3)
    stage3()
    product(1)
    across(3)
    weights(4)
    stage4()
    product(2)
    stage5()
    weights(5)
    across(4)
    product(3)
    stage6()
    weights(6)
    across(5)
    product(4)
    stage7()
    weights(7)
    across(6)
    product(5)
    stage8()
    across(7)
    product(6)
    across(8)
    product(7)
    stage9()
    product(8)
    stage10()
    finish()
    for copy in kept:
        copy.wait()
    pltpu.make_async_copy(outs.at[0], outs.at[0], rsem.at[BASE["out"]]).wait()
    moved = outs.at[pl.ds(0, 7)]
    got(moved, "outs")
    left(moved, "outs")
    left(tok.at[pl.ds(0, 7)], "tok")
    left(wts.reshape(4 * Z, half, width).at[pl.ds(0, 30)], "zp")
    left(part16, "s1")
    left(r2, "s2")
    left(nrm.at[pl.ds(0, 7)], "s3")
    left(r4, "s4")
    left(r5, "s5")
    left(r6, "s6")
    left(c7.at[pl.ds(0, 7)], "s7")
    left(c8.at[pl.ds(0, 3)], "s8")
    left(c8, "s9")
    left(c9, "s10")


def fused(lengths, inp, cot, frz, adn, aup):
    rows, width = cot.shape
    rank, features = adn.shape
    share = (features + width) // (2 * X)
    n = share // 6
    scratch = [
        pltpu.VMEM((2 * X, 2, rows // 2, width), BF16),
        pltpu.VMEM((Z, 2, 2, rows // 2, width), BF16),
        pltpu.VMEM((Z, 2 * X, rows, 2 * rows), BF16),
        pltpu.VMEM((rows, features), BF16),
        pltpu.VMEM((rows, width), BF16),
        pltpu.VMEM((rank, features), BF16),
        pltpu.VMEM((rank, width), BF16),
        pltpu.VMEM((4, 2 * rows, rank), BF16),
        pltpu.VMEM((X, rank, share), F32),
        pltpu.VMEM((X, rank, share), BF16),
        pltpu.VMEM((X, rank, share), BF16),
        pltpu.VMEM((X, rank, share), BF16),
        pltpu.VMEM((X - 1, rank, share), BF16),
        pltpu.VMEM((2, rank, share // 2), F32),
        pltpu.VMEM((2 * X, 8, 128), F32),
        pltpu.VMEM((rank, share // 2), F32),
        pltpu.VMEM((rank, share // 2), F32),
        pltpu.VMEM((Z, 8, n), F32),
        pltpu.VMEM((Z - 1, 8, n), F32),
        pltpu.VMEM((Z, 8, n), F32),
        pltpu.VMEM((X, 6, 8, n), F32),
        pltpu.VMEM((2, X, 6, 8, n), F32),
        pltpu.VMEM((2, 2, X, 6, 8, n), F32),
        pltpu.VMEM((rank, features), F32),
        pltpu.VMEM((rank, width), F32),
        pltpu.SemaphoreType.DMA((13,)),
        pltpu.SemaphoreType.DMA((TOTAL,)),
    ]
    anywhere = pl.BlockSpec(memory_space=pl.ANY)
    hbm = pl.BlockSpec(memory_space=pltpu.HBM)
    return pl.pallas_call(
        body,
        out_shape=(
            jax.ShapeDtypeStruct((rows, features), BF16),
            jax.ShapeDtypeStruct((rank, features), F32),
            jax.ShapeDtypeStruct((rank, width), F32),
        ),
        in_specs=[pl.BlockSpec(memory_space=pltpu.SMEM)] + [hbm] * 5,
        out_specs=(anywhere, anywhere, anywhere),
        scratch_shapes=scratch,
        compiler_params=pltpu.CompilerParams(
            collective_id=0, has_side_effects=True, vmem_limit_bytes=44 << 20
        ),
    )(lengths, *(pltpu.with_memory_space_constraint(a, pltpu.HBM) for a in (inp, cot, frz, adn, aup)))


def close(lengths, raw, gd, gu, og_out, gd_out, gu_out, masked, sem):
    copies = [
        pltpu.make_async_copy(gd, gd_out, sem.at[0]),
        pltpu.make_async_copy(gu, gu_out, sem.at[1]),
    ]
    rows = raw.shape[0]
    n = masked.shape[1]
    for i in range(rows // n):
        at = pl.ds(i * n, n)
        position = lax.axis_index("ctx") * rows + i * n
        position = position + lax.broadcasted_iota(jnp.int32, (n, 1), 0)
        masked[i] = jnp.where(position < lengths[0], raw[at, :], jnp.zeros((), BF16))
        copies.append(pltpu.make_async_copy(masked.at[i], og_out.at[at], sem.at[2 + i]))
        copies[-1].start()
        if i == 0:
            for copy in copies[:2]:
                copy.start()
    for copy in copies:
        copy.wait()


def shard(inputs, cotangent, lengths, frozen, adapter_down, adapter_up):
    _, rows, features = inputs.shape
    results = fused(lengths, inputs[0], cotangent[0], frozen, adapter_down, adapter_up)
    vmem = pl.BlockSpec(memory_space=pltpu.VMEM)
    hbm = pl.BlockSpec(memory_space=pltpu.HBM)
    n = 16
    input_grads, grad_down, grad_up = pl.pallas_call(
        close,
        out_shape=[jax.ShapeDtypeStruct(r.shape, r.dtype) for r in results],
        in_specs=[pl.BlockSpec(memory_space=pltpu.SMEM)] + [vmem] * 3,
        out_specs=[hbm] * 3,
        scratch_shapes=[
            pltpu.VMEM((rows // n, n, features), BF16),
            pltpu.SemaphoreType.DMA((2 + rows // n,)),
        ],
        compiler_params=pltpu.CompilerParams(vmem_limit_bytes=16 << 20),
    )(lengths, *results)
    return input_grads[None], grad_down, grad_up


def solution(mesh):
    rows = P(("dp", "fsdp"), "ctx", None)
    return jax.shard_map(
        shard,
        mesh=mesh,
        in_specs=(rows, rows, P(("dp", "fsdp")), P(("fsdp", "ctx"), None), P(), P()),
        out_specs=(rows, P(), P()),
        check_vma=False,
    )
```

```python
import functools
import math

import jax
import jax.numpy as jnp
from jax import lax
from jax.experimental import pallas as pl
from jax.experimental.pallas import tpu as pltpu
from jax.sharding import PartitionSpec as P

MESH = pl.DeviceIdType.MESH
BF16, F32 = jnp.bfloat16, jnp.float32
X, Z = 4, 8
OFFSETS = (0, -1, 1, -2, 2, -3, 3, 4)
SEMS = dict(
    local=6, tok=4, tok2=2, mate=7, zp=7, zm=7, cross=8, pair=8, out=1, outs=1,
    s1=1, s2=1, s3=1, s4=1, s5=1, s6=1, s7=1, s8=1, s9=1, s10=1,
)
BASE, TOTAL = {}, 0
for _name, _count in SEMS.items():
    BASE[_name] = TOTAL
    TOTAL += _count
GROUP = dict(tok=0, tok2=0, mate=0, zp=1, zm=1, cross=1, pair=1, outs=2)
GROUP.update({f"s{i}": i + 2 for i in range(1, 11)})


def last(a, b):
    return lax.dot_general(a, b, (((1,), (1,)), ((), ())), preferred_element_type=F32)


def wrap(value, size):
    return lax.rem(value + size, size)


def body(
    lengths, inp, cot, frz, adn, aup,
    og, gd_out, gu_out,
    tok, wts, outs, xin, cotv, dn, up, low2,
    part, part16, q16, r1, r2, share, nrm, r4, r6, g8, r5, c7, c8, c9, c10, gd, gu,
    ssem, rsem,
):
    dp, fsdp, ctx = (lax.axis_index(n) for n in ("dp", "fsdp", "ctx"))
    lo, z, c, x, hi = dp, fsdp // 2, lax.rem(fsdp, 2), ctx // 2, lax.rem(ctx, 2)
    rows, width = cot.shape
    half = rows // 2

    def dev(dx=0, dz=0, dc=0, flip_hi=0, flip_lo=0):
        xx, zz = wrap(x + dx, X), wrap(z + dz, Z)
        cc = 1 - c if dc else c
        hh = 1 - hi if flip_hi else hi
        ll = 1 - lo if flip_lo else lo
        return (ll, zz * 2 + cc, xx * 2 + hh)

    peers = [dict(dx=1), dict(dx=-1), dict(dz=1), dict(dz=-1), dict(dc=1)]
    peers += [dict(flip_hi=1), dict(flip_lo=1), dict(flip_hi=1, flip_lo=1)]

    def send(src, dst, name, i, **to):
        r = BASE[name] + min(i, SEMS[name] - 1)
        pltpu.make_async_remote_copy(
            src, dst, ssem.at[GROUP[name]], rsem.at[r], device_id=dev(**to), device_id_type=MESH
        ).start()

    def got(dst, name, i=0):
        pltpu.make_async_remote_copy(
            dst, dst, ssem.at[GROUP[name]], rsem.at[BASE[name] + i],
            device_id=dev(dc=1), device_id_type=MESH,
        ).wait_recv()

    def left(src, name):
        pltpu.make_async_remote_copy(
            src, src, ssem.at[GROUP[name]], rsem.at[BASE[name]],
            device_id=dev(dc=1), device_id_type=MESH,
        ).wait_send()

    def local(src, dst, i):
        copy = pltpu.make_async_copy(src, dst, rsem.at[BASE["local"] + i])
        copy.start()
        return copy

    own = x * 2 + c

    def slot(dx, dc=0):
        return wrap(x + dx, X) * 2 + (1 - c if dc else c)

    def wz(d):
        return wrap(z + d, Z)

    cot2, frz2 = cot.reshape(2, half, width), frz.reshape(2, half, width)

    loads = [
        local(aup, up, 0),
        local(cot2, tok.at[own], 1),
        local(adn, dn, 2),
        local(inp, xin, 3),
        local(frz2, wts.at[z, hi], 4),
        local(cot, cotv, 5),
    ]
    barrier = pltpu.get_barrier_semaphore()
    for p in peers:
        pl.semaphore_signal(barrier, inc=1, device_id=dev(**p), device_id_type=MESH)
    pl.semaphore_wait(barrier, len(peers))

    send(cot2.at[0], tok.at[own, 0], "tok", 0, dx=1)
    send(cot2.at[1], tok.at[own, 1], "tok", 3, dx=-1)
    send(frz2.at[lo], wts.at[z, hi, lo], "zp", 0, dz=1)
    send(frz2.at[lo], wts.at[z, hi, lo], "zm", 0, dz=-1)
    send(frz2.at[lo], wts.at[z, hi, lo], "cross", 0, flip_hi=1, flip_lo=1)
    send(cot2.at[1], tok.at[own, 1], "tok", 1, dx=1)
    send(cot2.at[0], tok.at[own, 0], "tok", 2, dx=-1)
    send(frz2.at[1 - lo], wts.at[z, hi, 1 - lo], "zp", 1, dz=1)
    send(frz2.at[1 - lo], wts.at[z, hi, 1 - lo], "zm", 1, dz=-1)
    send(cot2, tok.at[own], "mate", 0, dc=1)

    def partials():
        for i in (0, 5, 2, 3):
            loads[i].wait()
        position = ctx * rows + lax.broadcasted_iota(jnp.int32, (1, rows), 1)
        live = position < lengths[0]
        mine = cotv[...]
        lowered = jnp.where(live, last(up[...], mine), 0.0).astype(BF16)
        proj = jnp.where(live, last(dn[...], xin[...]), 0.0).astype(BF16)
        dcol, ucol = xin.shape[1] // (2 * X), width // (2 * X)
        for i in range(2 * X):
            j, keep = (i % X) * 2 + ((1 - hi) if i < X else hi), i >= X
            a = xin[:, pl.ds(pl.multiple_of(j * dcol, dcol), dcol)]
            pd = 2.0 * jnp.dot(lowered, a, preferred_element_type=F32)
            b = cotv[:, pl.ds(pl.multiple_of(j * ucol, ucol), ucol)]
            pu = 2.0 * jnp.dot(proj, b, preferred_element_type=F32)
            to = part if keep else part16
            to[i % X, :, :dcol] = pd.astype(to.dtype)
            to[i % X, :, dcol:] = pu.astype(to.dtype)
            if i == X - 1:
                send(part16, r1, "s1", 0, flip_hi=1)

    def stage2():
        got(r1, "s1", 0)
        part[...] = part[...] + r1[...].astype(F32)
        q16[...] = part[...].astype(BF16)
        for dx in range(1, X):
            send(q16.at[wrap(x + dx, X)], r2.at[dx - 1], "s2", dx - 1, dx=dx)

    def stage3():
        got(r2, "s2")
        total = part[x]
        for i in range(X - 1):
            total = total + r2[i].astype(F32)
        n = total.shape[1] // 2
        share[0] = total[:, :n]
        share[1] = total[:, n:]
        square = jnp.sum(jnp.sum(total * total, axis=1, keepdims=True), axis=0, keepdims=True)
        nrm[ctx] = jnp.broadcast_to(square, nrm.shape[1:])
        for i in range(1, 2 * X):
            send(nrm.at[ctx], nrm.at[ctx], "s3", i - 1, dx=i // 2, flip_hi=i % 2)

    def stage4():
        got(nrm.at[pl.ds(0, 7)], "s3")
        square = nrm[0]
        for i in range(1, 2 * X):
            square = square + nrm[i]
        bound = 10.0 * math.sqrt(dn.shape[0] * (xin.shape[1] + width))
        factor = (bound / jnp.maximum(jnp.sqrt(square), bound))[:1, :1]
        share[...] = share[...] * factor.reshape(1, 1, 1)
        send(share.at[1 - c], r4, "s4", 0, dc=1)

    def stage5():
        got(r4, "s4", 0)
        share[c] = share[c] + r4[...]
        send(share.at[c], r6, "s6", 0, flip_lo=1)

    def stage6():
        got(r6, "s6", 0)
        both = share[c] + r6[...]
        n = g8.shape[2]
        for o in range(Z):
            if o < 6:
                g8[o] = both[(o % 2) * 8 : (o % 2) * 8 + 8, (o // 2) * n : (o // 2 + 1) * n]
            else:
                g8[o] = jnp.zeros(g8.shape[1:], F32)
        for dz in range(1, Z):
            send(g8.at[wz(dz)], r5.at[dz - 1], "s5", dz - 1, dz=dz)

    def stage7():
        got(r5, "s5")
        total = g8[z]
        for dz in range(1, Z):
            total = total + r5[dz - 1]
        c7[z] = total * (1.0 / 32.0)
        for dz in range(1, Z):
            send(c7.at[z], c7.at[z], "s7", dz - 1, dz=dz)

    def stage8():
        got(c7.at[pl.ds(0, 7)], "s7")
        c8[x] = c7[:6]
        for dx in range(1, X):
            send(c7.at[pl.ds(0, 6)], c8.at[x], "s8", dx - 1, dx=dx)

    def stage9():
        got(c8.at[pl.ds(0, 3)], "s8")
        c9[hi] = c8[...]
        send(c8, c9.at[hi], "s9", 0, flip_hi=1, flip_lo=1)

    def stage10():
        got(c9.at[1 - hi], "s9", 0)
        c10[c] = c9[...]
        send(c9, c10.at[c], "s10", 0, dc=1)

    def finish():
        got(c10.at[1 - c], "s10", 0)
        n = g8.shape[2]
        dcol, ucol = xin.shape[1] // (2 * X), width // (2 * X)
        for j in range(2 * X):
            for cc in range(2):
                for o in range(6):
                    r = slice((o % 2) * 8, (o % 2) * 8 + 8)
                    v = c10[cc, j % 2, j // 2, o]
                    at = cc * 3 * n + (o // 2) * n
                    k = max(0, min(n, dcol - at))
                    if k:
                        gd[r, j * dcol + at : j * dcol + at + k] = v[:, :k]
                    if k < n:
                        u = at + k - dcol
                        gu[r, j * ucol + u : j * ucol + u + n - k] = v[:, k:]
        step = xin.shape[1] // 4
        for i in range(4):
            at = pl.ds(i * step, step)
            kept.append(local(gd.at[:, at], gd_out.at[:, at], i))
        kept.append(local(gu, gu_out, 4))

    def weights(k):
        d, which = (k + 1) // 2, (lo if k % 2 else 1 - lo)
        at = wts.at[wz(-d), hi, which]
        got(at, "zp", k - 1)
        if k <= 5:
            send(at, at, "zp", k + 1, dz=1)
        if k % 2:
            send(at, at, "cross", OFFSETS.index(-d if d < 4 else 4), flip_hi=1, flip_lo=1)
        if k == 7:
            which = 1 - lo
        at = wts.at[wz(d), hi, which]
        got(at, "zm", k - 1)
        if k <= 4:
            send(at, at, "zm", k + 1, dz=-1)
        if k == 6:
            send(at, at, "zm", 6, dz=-1)
        if k % 2 and k < 7:
            send(at, at, "cross", OFFSETS.index(d), flip_hi=1, flip_lo=1)

    def across(k):
        at = wts.at[wz(OFFSETS[k - 1]), 1 - hi, 1 - lo]
        got(at, "cross", k - 1)
        send(at, at, "pair", k - 1, flip_lo=1)

    def tokens(k):
        if k == 3:
            moved = ((slot(2), 0, "tok2", 0), (slot(2), 1, "tok2", 1))
        else:
            a, b = (0, 1) if k == 1 else (1, 0)
            moved = ((slot(-1), a, "tok", a), (slot(1), b, "tok", 2 + b))
        for i, (s, part_, name, index) in enumerate(moved):
            at = tok.at[s, part_]
            got(at, name, index)
            send(at, at, "mate", 1 + 2 * (k - 1) + i, dc=1)
            if k == 1:
                send(at, at, "tok2", i, dx=1 if i == 0 else -1)

    kept = []

    def lower(dx):
        if dx == 0:
            loads[1].wait()
            got(tok.at[slot(0, 1)], "mate", 0)
        elif dx == 2:
            got(tok.at[slot(2, 1), 0], "mate", 5)
            got(tok.at[slot(2, 1), 1], "mate", 6)
        else:
            k = 0 if dx == 3 else 1
            got(tok.at[slot(dx, 1), k], "mate", 1 + k)
            got(tok.at[slot(dx, 1), 1 - k], "mate", 3 + k)
        xx = wrap(x + dx, X)
        t = tok[pl.ds(xx * 2, 2)].reshape(2 * rows, width)
        lowered = last(t, up[...]).astype(BF16)
        low2[xx] = lowered + lowered

    def chunk(i, dx, cols):
        shard, xx = wz(OFFSETS[i - 1]), wrap(x + dx, X)
        t = tok[pl.ds(xx * 2, 2)].reshape(2 * rows, width)
        value = last(t, wts[shard].reshape(2 * rows, width))
        value = value + jnp.dot(low2[xx], dn[:, cols], preferred_element_type=F32)
        outs[i - 1, pl.ds(xx * 2, 2)] = value.astype(BF16).reshape(2, rows, 2 * rows)

    def deliver(i, dx, dc, cols):
        return pltpu.make_async_remote_copy(
            outs.at[i - 1, slot(dx, dc)], og.at[:, cols],
            ssem.at[GROUP["outs"]], rsem.at[BASE["outs"]],
            device_id=dev(dx=dx, dc=dc), device_id_type=MESH,
        )

    def product(i):
        if i == 1:
            loads[4].wait()
        shard = wz(OFFSETS[i - 1])
        got(wts.at[shard, 1 - hi, lo], "pair", i - 1)
        at = pl.multiple_of(((shard * 2 + c) * 8 + x * 2) * rows, 2 * rows)
        cols = pl.ds(at, 2 * rows)
        if i == 1:
            for dx in (1, 3, 2, 0):
                if dx == 2:
                    lower(2)
                chunk(i, dx, cols)
                if dx:
                    for dc in range(2):
                        deliver(i, dx, dc, cols).start()
        else:

            @pl.loop(0, 3)
            def _(t):
                dx = 2 - t + 3 * (t // 2)
                chunk(i, dx, cols)
                for dc in range(2):
                    deliver(i, dx, dc, cols).start()

            chunk(i, 0, cols)
        deliver(i, 0, 1, cols).start()
        pltpu.make_async_copy(outs.at[i - 1, own], og.at[:, cols], rsem.at[BASE["out"]]).start()

    partials()
    tokens(1)
    weights(1)
    stage2()
    tokens(2)
    across(1)
    weights(2)
    lower(0)
    lower(1)
    lower(3)
    across(2)
    weights(3)
    tokens(3)
    stage3()
    product(1)
    across(3)
    weights(4)
    stage4()
    product(2)
    stage5()
    weights(5)
    across(4)
    product(3)
    stage6()
    weights(6)
    across(5)
    product(4)
    stage7()
    weights(7)
    across(6)
    product(5)
    stage8()
    across(7)
    product(6)
    across(8)
    product(7)
    stage9()
    product(8)
    stage10()
    finish()
    for copy in kept:
        copy.wait()
    pltpu.make_async_copy(outs.at[0], outs.at[0], rsem.at[BASE["out"]]).wait()
    moved = outs.at[pl.ds(0, 7)]
    got(moved, "outs")
    left(moved, "outs")
    left(tok.at[pl.ds(0, 7)], "tok")
    left(wts.reshape(4 * Z, half, width).at[pl.ds(0, 30)], "zp")
    left(part16, "s1")
    left(r2, "s2")
    left(nrm.at[pl.ds(0, 7)], "s3")
    left(r4, "s4")
    left(r5, "s5")
    left(r6, "s6")
    left(c7.at[pl.ds(0, 7)], "s7")
    left(c8.at[pl.ds(0, 3)], "s8")
    left(c8, "s9")
    left(c9, "s10")


def fused(lengths, inp, cot, frz, adn, aup):
    rows, width = cot.shape
    rank, features = adn.shape
    share = (features + width) // (2 * X)
    n = share // 6
    scratch = [
        pltpu.VMEM((2 * X, 2, rows // 2, width), BF16),
        pltpu.VMEM((Z, 2, 2, rows // 2, width), BF16),
        pltpu.VMEM((Z, 2 * X, rows, 2 * rows), BF16),
        pltpu.VMEM((rows, features), BF16),
        pltpu.VMEM((rows, width), BF16),
        pltpu.VMEM((rank, features), BF16),
        pltpu.VMEM((rank, width), BF16),
        pltpu.VMEM((4, 2 * rows, rank), BF16),
        pltpu.VMEM((X, rank, share), F32),
        pltpu.VMEM((X, rank, share), BF16),
        pltpu.VMEM((X, rank, share), BF16),
        pltpu.VMEM((X, rank, share), BF16),
        pltpu.VMEM((X - 1, rank, share), BF16),
        pltpu.VMEM((2, rank, share // 2), F32),
        pltpu.VMEM((2 * X, 8, 128), F32),
        pltpu.VMEM((rank, share // 2), F32),
        pltpu.VMEM((rank, share // 2), F32),
        pltpu.VMEM((Z, 8, n), F32),
        pltpu.VMEM((Z - 1, 8, n), F32),
        pltpu.VMEM((Z, 8, n), F32),
        pltpu.VMEM((X, 6, 8, n), F32),
        pltpu.VMEM((2, X, 6, 8, n), F32),
        pltpu.VMEM((2, 2, X, 6, 8, n), F32),
        pltpu.VMEM((rank, features), F32),
        pltpu.VMEM((rank, width), F32),
        pltpu.SemaphoreType.DMA((13,)),
        pltpu.SemaphoreType.DMA((TOTAL,)),
    ]
    anywhere = pl.BlockSpec(memory_space=pl.ANY)
    hbm = pl.BlockSpec(memory_space=pltpu.HBM)
    return pl.pallas_call(
        body,
        out_shape=(
            jax.ShapeDtypeStruct((rows, features), BF16),
            jax.ShapeDtypeStruct((rank, features), F32),
            jax.ShapeDtypeStruct((rank, width), F32),
        ),
        in_specs=[pl.BlockSpec(memory_space=pltpu.SMEM)] + [hbm] * 5,
        out_specs=(anywhere, anywhere, anywhere),
        scratch_shapes=scratch,
        compiler_params=pltpu.CompilerParams(
            collective_id=0, has_side_effects=True, vmem_limit_bytes=44 << 20
        ),
    )(lengths, *(pltpu.with_memory_space_constraint(a, pltpu.HBM) for a in (inp, cot, frz, adn, aup)))


def close(lengths, raw, gd, gu, og_out, gd_out, gu_out, masked, sem):
    copies = [
        pltpu.make_async_copy(gd, gd_out, sem.at[0]),
        pltpu.make_async_copy(gu, gu_out, sem.at[1]),
    ]
    rows = raw.shape[0]
    n = masked.shape[1]
    for i in range(rows // n):
        at = pl.ds(i * n, n)
        position = lax.axis_index("ctx") * rows + i * n
        position = position + lax.broadcasted_iota(jnp.int32, (n, 1), 0)
        masked[i] = jnp.where(position < lengths[0], raw[at, :], jnp.zeros((), BF16))
        copies.append(pltpu.make_async_copy(masked.at[i], og_out.at[at], sem.at[2 + i]))
        copies[-1].start()
        if i == 0:
            for copy in copies[:2]:
                copy.start()
    for copy in copies:
        copy.wait()


def shard(inputs, cotangent, lengths, frozen, adapter_down, adapter_up):
    _, rows, features = inputs.shape
    results = fused(lengths, inputs[0], cotangent[0], frozen, adapter_down, adapter_up)
    vmem = pl.BlockSpec(memory_space=pltpu.VMEM)
    hbm = pl.BlockSpec(memory_space=pltpu.HBM)
    n = 16
    input_grads, grad_down, grad_up = pl.pallas_call(
        close,
        out_shape=[jax.ShapeDtypeStruct(r.shape, r.dtype) for r in results],
        in_specs=[pl.BlockSpec(memory_space=pltpu.SMEM)] + [vmem] * 3,
        out_specs=[hbm] * 3,
        scratch_shapes=[
            pltpu.VMEM((rows // n, n, features), BF16),
            pltpu.SemaphoreType.DMA((2 + rows // n,)),
        ],
        compiler_params=pltpu.CompilerParams(vmem_limit_bytes=16 << 20),
    )(lengths, *results)
    return input_grads[None], grad_down, grad_up


def solution(mesh):
    rows = P(("dp", "fsdp"), "ctx", None)
    return jax.shard_map(
        shard,
        mesh=mesh,
        in_specs=(rows, rows, P(("dp", "fsdp")), P(("fsdp", "ctx"), None), P(), P()),
        out_specs=(rows, P(), P()),
        check_vma=False,
    )
```

```python
import functools
import math

import jax
import jax.numpy as jnp
from jax import lax
from jax.experimental import pallas as pl
from jax.experimental.pallas import tpu as pltpu
from jax.sharding import PartitionSpec as P

MESH = pl.DeviceIdType.MESH
BF16, F32 = jnp.bfloat16, jnp.float32
X, Z = 4, 8
OFFSETS = (0, -1, 1, -2, 2, -3, 3, 4)
SEMS = dict(
    local=6, tok=4, tok2=2, mate=7, zp=7, zm=7, cross=8, pair=8, out=1, outs=1,
    s1=1, s2=1, s3=1, s4=1, s5=1, s6=1, s7=1, s8=1, s9=1, s10=1,
)
BASE, TOTAL = {}, 0
for _name, _count in SEMS.items():
    BASE[_name] = TOTAL
    TOTAL += _count
GROUP = dict(tok=0, tok2=0, mate=0, zp=1, zm=1, cross=1, pair=1, outs=2)
GROUP.update({f"s{i}": i + 2 for i in range(1, 11)})


def last(a, b):
    return lax.dot_general(a, b, (((1,), (1,)), ((), ())), preferred_element_type=F32)


def wrap(value, size):
    return lax.rem(value + size, size)


def body(
    lengths, inp, cot, frz, adn, aup,
    og, gd_out, gu_out,
    tok, wts, outs, xin, cotv, dn, up, low2,
    part, part16, q16, r1, r2, share, nrm, r4, r6, g8, r5, c7, c8, c9, c10, gd, gu,
    ssem, rsem,
):
    dp, fsdp, ctx = (lax.axis_index(n) for n in ("dp", "fsdp", "ctx"))
    lo, z, c, x, hi = dp, fsdp // 2, lax.rem(fsdp, 2), ctx // 2, lax.rem(ctx, 2)
    rows, width = cot.shape
    half = rows // 2

    def dev(dx=0, dz=0, dc=0, flip_hi=0, flip_lo=0):
        xx, zz = wrap(x + dx, X), wrap(z + dz, Z)
        cc = 1 - c if dc else c
        hh = 1 - hi if flip_hi else hi
        ll = 1 - lo if flip_lo else lo
        return (ll, zz * 2 + cc, xx * 2 + hh)

    peers = [dict(dx=1), dict(dx=-1), dict(dz=1), dict(dz=-1), dict(dc=1)]
    peers += [dict(flip_hi=1), dict(flip_lo=1), dict(flip_hi=1, flip_lo=1)]

    def send(src, dst, name, i, **to):
        r = BASE[name] + min(i, SEMS[name] - 1)
        pltpu.make_async_remote_copy(
            src, dst, ssem.at[GROUP[name]], rsem.at[r], device_id=dev(**to), device_id_type=MESH
        ).start()

    def got(dst, name, i=0):
        pltpu.make_async_remote_copy(
            dst, dst, ssem.at[GROUP[name]], rsem.at[BASE[name] + i],
            device_id=dev(dc=1), device_id_type=MESH,
        ).wait_recv()

    def left(src, name):
        pltpu.make_async_remote_copy(
            src, src, ssem.at[GROUP[name]], rsem.at[BASE[name]],
            device_id=dev(dc=1), device_id_type=MESH,
        ).wait_send()

    def local(src, dst, i):
        copy = pltpu.make_async_copy(src, dst, rsem.at[BASE["local"] + i])
        copy.start()
        return copy

    own = x * 2 + c

    def slot(dx, dc=0):
        return wrap(x + dx, X) * 2 + (1 - c if dc else c)

    def wz(d):
        return wrap(z + d, Z)

    cot2, frz2 = cot.reshape(2, half, width), frz.reshape(2, half, width)

    loads = [
        local(aup, up, 0),
        local(cot2, tok.at[own], 1),
        local(adn, dn, 2),
        local(inp, xin, 3),
        local(frz2, wts.at[z, hi], 4),
        local(cot, cotv, 5),
    ]
    barrier = pltpu.get_barrier_semaphore()
    for p in peers:
        pl.semaphore_signal(barrier, inc=1, device_id=dev(**p), device_id_type=MESH)
    pl.semaphore_wait(barrier, len(peers))

    send(cot2.at[0], tok.at[own, 0], "tok", 0, dx=1)
    send(cot2.at[1], tok.at[own, 1], "tok", 3, dx=-1)
    send(frz2.at[lo], wts.at[z, hi, lo], "zp", 0, dz=1)
    send(frz2.at[lo], wts.at[z, hi, lo], "zm", 0, dz=-1)
    send(frz2.at[lo], wts.at[z, hi, lo], "cross", 0, flip_hi=1, flip_lo=1)
    send(cot2.at[1], tok.at[own, 1], "tok", 1, dx=1)
    send(cot2.at[0], tok.at[own, 0], "tok", 2, dx=-1)
    send(frz2.at[1 - lo], wts.at[z, hi, 1 - lo], "zp", 1, dz=1)
    send(frz2.at[1 - lo], wts.at[z, hi, 1 - lo], "zm", 1, dz=-1)
    send(cot2, tok.at[own], "mate", 0, dc=1)

    def partials():
        for i in (0, 5, 2, 3):
            loads[i].wait()
        position = ctx * rows + lax.broadcasted_iota(jnp.int32, (1, rows), 1)
        live = position < lengths[0]
        mine = cotv[...]
        lowered = jnp.where(live, last(up[...], mine), 0.0).astype(BF16)
        proj = jnp.where(live, last(dn[...], xin[...]), 0.0).astype(BF16)
        dcol, ucol = xin.shape[1] // (2 * X), width // (2 * X)
        for i in range(2 * X):
            j, keep = (i % X) * 2 + ((1 - hi) if i < X else hi), i >= X
            a = xin[:, pl.ds(pl.multiple_of(j * dcol, dcol), dcol)]
            pd = 2.0 * jnp.dot(lowered, a, preferred_element_type=F32)
            b = cotv[:, pl.ds(pl.multiple_of(j * ucol, ucol), ucol)]
            pu = 2.0 * jnp.dot(proj, b, preferred_element_type=F32)
            to = part if keep else part16
            to[i % X, :, :dcol] = pd.astype(to.dtype)
            to[i % X, :, dcol:] = pu.astype(to.dtype)
            if i == X - 1:
                send(part16, r1, "s1", 0, flip_hi=1)

    def stage2():
        got(r1, "s1", 0)
        part[...] = part[...] + r1[...].astype(F32)
        q16[...] = part[...].astype(BF16)
        for dx in range(1, X):
            send(q16.at[wrap(x + dx, X)], r2.at[dx - 1], "s2", dx - 1, dx=dx)

    def stage3():
        got(r2, "s2")
        total = part[x]
        for i in range(X - 1):
            total = total + r2[i].astype(F32)
        n = total.shape[1] // 2
        share[0] = total[:, :n]
        share[1] = total[:, n:]
        square = jnp.sum(jnp.sum(total * total, axis=1, keepdims=True), axis=0, keepdims=True)
        nrm[ctx] = jnp.broadcast_to(square, nrm.shape[1:])
        for i in range(1, 2 * X):
            send(nrm.at[ctx], nrm.at[ctx], "s3", i - 1, dx=i // 2, flip_hi=i % 2)

    def stage4():
        got(nrm.at[pl.ds(0, 7)], "s3")
        square = nrm[0]
        for i in range(1, 2 * X):
            square = square + nrm[i]
        bound = 10.0 * math.sqrt(dn.shape[0] * (xin.shape[1] + width))
        factor = (bound / jnp.maximum(jnp.sqrt(square), bound))[:1, :1]
        share[...] = share[...] * factor.reshape(1, 1, 1)
        send(share.at[1 - c], r4, "s4", 0, dc=1)

    def stage5():
        got(r4, "s4", 0)
        share[c] = share[c] + r4[...]
        send(share.at[c], r6, "s6", 0, flip_lo=1)

    def stage6():
        got(r6, "s6", 0)
        both = share[c] + r6[...]
        n = g8.shape[2]
        for o in range(Z):
            if o < 6:
                g8[o] = both[(o % 2) * 8 : (o % 2) * 8 + 8, (o // 2) * n : (o // 2 + 1) * n]
            else:
                g8[o] = jnp.zeros(g8.shape[1:], F32)
        for dz in range(1, Z):
            send(g8.at[wz(dz)], r5.at[dz - 1], "s5", dz - 1, dz=dz)

    def stage7():
        got(r5, "s5")
        total = g8[z]
        for dz in range(1, Z):
            total = total + r5[dz - 1]
        c7[x] = total * (1.0 / 32.0)
        for dx in range(1, X):
            send(c7.at[x], c7.at[x], "s8", dx - 1, dx=dx)

    def stage8():
        got(c7.at[pl.ds(0, 3)], "s8")
        c8[z] = c7[...]
        for dz in range(1, Z):
            send(c7, c8.at[z], "s7", dz - 1, dz=dz)

    def stage9():
        got(c8.at[pl.ds(0, 7)], "s7")
        six = c8.at[pl.ds(0, 6)]
        c9[hi] = six[...]
        send(six, c9.at[hi], "s9", 0, flip_hi=1, flip_lo=1)

    def stage10():
        got(c9.at[1 - hi], "s9", 0)
        c10[c] = c9[...]
        send(c9, c10.at[c], "s10", 0, dc=1)

    def finish():
        got(c10.at[1 - c], "s10", 0)
        n = g8.shape[2]
        dcol, ucol = xin.shape[1] // (2 * X), width // (2 * X)
        for j in range(2 * X):
            for cc in range(2):
                for o in range(6):
                    r = slice((o % 2) * 8, (o % 2) * 8 + 8)
                    v = c10[cc, j % 2, o, j // 2]
                    at = cc * 3 * n + (o // 2) * n
                    k = max(0, min(n, dcol - at))
                    if k:
                        gd[r, j * dcol + at : j * dcol + at + k] = v[:, :k]
                    if k < n:
                        u = at + k - dcol
                        gu[r, j * ucol + u : j * ucol + u + n - k] = v[:, k:]
        step = xin.shape[1] // 4
        for i in range(4):
            at = pl.ds(i * step, step)
            kept.append(local(gd.at[:, at], gd_out.at[:, at], i))
        kept.append(local(gu, gu_out, 4))

    def weights(k):
        d, which = (k + 1) // 2, (lo if k % 2 else 1 - lo)
        at = wts.at[wz(-d), hi, which]
        got(at, "zp", k - 1)
        if k <= 5:
            send(at, at, "zp", k + 1, dz=1)
        if k % 2:
            send(at, at, "cross", OFFSETS.index(-d if d < 4 else 4), flip_hi=1, flip_lo=1)
        if k == 7:
            which = 1 - lo
        at = wts.at[wz(d), hi, which]
        got(at, "zm", k - 1)
        if k <= 4:
            send(at, at, "zm", k + 1, dz=-1)
        if k == 6:
            send(at, at, "zm", 6, dz=-1)
        if k % 2 and k < 7:
            send(at, at, "cross", OFFSETS.index(d), flip_hi=1, flip_lo=1)

    def across(k):
        at = wts.at[wz(OFFSETS[k - 1]), 1 - hi, 1 - lo]
        got(at, "cross", k - 1)
        send(at, at, "pair", k - 1, flip_lo=1)

    def tokens(k):
        if k == 3:
            moved = ((slot(2), 0, "tok2", 0), (slot(2), 1, "tok2", 1))
        else:
            a, b = (0, 1) if k == 1 else (1, 0)
            moved = ((slot(-1), a, "tok", a), (slot(1), b, "tok", 2 + b))
        for i, (s, part_, name, index) in enumerate(moved):
            at = tok.at[s, part_]
            got(at, name, index)
            send(at, at, "mate", 1 + 2 * (k - 1) + i, dc=1)
            if k == 1:
                send(at, at, "tok2", i, dx=1 if i == 0 else -1)

    kept = []

    def lower(dx):
        if dx == 0:
            loads[1].wait()
            got(tok.at[slot(0, 1)], "mate", 0)
        elif dx == 2:
            got(tok.at[slot(2, 1), 0], "mate", 5)
            got(tok.at[slot(2, 1), 1], "mate", 6)
        else:
            k = 0 if dx == 3 else 1
            got(tok.at[slot(dx, 1), k], "mate", 1 + k)
            got(tok.at[slot(dx, 1), 1 - k], "mate", 3 + k)
        xx = wrap(x + dx, X)
        t = tok[pl.ds(xx * 2, 2)].reshape(2 * rows, width)
        lowered = last(t, up[...]).astype(BF16)
        low2[xx] = lowered + lowered

    def chunk(i, dx, cols):
        shard, xx = wz(OFFSETS[i - 1]), wrap(x + dx, X)
        t = tok[pl.ds(xx * 2, 2)].reshape(2 * rows, width)
        value = last(t, wts[shard].reshape(2 * rows, width))
        value = value + jnp.dot(low2[xx], dn[:, cols], preferred_element_type=F32)
        outs[i - 1, pl.ds(xx * 2, 2)] = value.astype(BF16).reshape(2, rows, 2 * rows)

    def deliver(i, dx, dc, cols):
        return pltpu.make_async_remote_copy(
            outs.at[i - 1, slot(dx, dc)], og.at[:, cols],
            ssem.at[GROUP["outs"]], rsem.at[BASE["outs"]],
            device_id=dev(dx=dx, dc=dc), device_id_type=MESH,
        )

    def product(i):
        if i == 1:
            loads[4].wait()
        shard = wz(OFFSETS[i - 1])
        got(wts.at[shard, 1 - hi, lo], "pair", i - 1)
        at = pl.multiple_of(((shard * 2 + c) * 8 + x * 2) * rows, 2 * rows)
        cols = pl.ds(at, 2 * rows)
        if i == 1:
            for dx in (1, 3, 2, 0):
                if dx == 2:
                    lower(2)
                chunk(i, dx, cols)
                if dx:
                    for dc in range(2):
                        deliver(i, dx, dc, cols).start()
        else:

            @pl.loop(0, 3)
            def _(t):
                dx = 2 - t + 3 * (t // 2)
                chunk(i, dx, cols)
                for dc in range(2):
                    deliver(i, dx, dc, cols).start()

            chunk(i, 0, cols)
        deliver(i, 0, 1, cols).start()
        pltpu.make_async_copy(outs.at[i - 1, own], og.at[:, cols], rsem.at[BASE["out"]]).start()

    partials()
    tokens(1)
    weights(1)
    stage2()
    tokens(2)
    across(1)
    weights(2)
    lower(0)
    lower(1)
    lower(3)
    across(2)
    weights(3)
    tokens(3)
    stage3()
    product(1)
    across(3)
    weights(4)
    stage4()
    product(2)
    stage5()
    weights(5)
    across(4)
    product(3)
    stage6()
    weights(6)
    across(5)
    product(4)
    stage7()
    weights(7)
    across(6)
    product(5)
    across(7)
    stage8()
    product(6)
    across(8)
    product(7)
    stage9()
    product(8)
    stage10()
    finish()
    for copy in kept:
        copy.wait()
    pltpu.make_async_copy(outs.at[0], outs.at[0], rsem.at[BASE["out"]]).wait()
    moved = outs.at[pl.ds(0, 7)]
    got(moved, "outs")
    left(moved, "outs")
    left(tok.at[pl.ds(0, 7)], "tok")
    left(wts.reshape(4 * Z, half, width).at[pl.ds(0, 30)], "zp")
    left(part16, "s1")
    left(r2, "s2")
    left(nrm.at[pl.ds(0, 7)], "s3")
    left(r4, "s4")
    left(r5, "s5")
    left(r6, "s6")
    left(c8.at[pl.ds(0, 7)], "s7")
    left(c7.at[pl.ds(0, 3)], "s8")
    left(c8.at[pl.ds(0, 6)], "s9")
    left(c9, "s10")


def fused(lengths, inp, cot, frz, adn, aup):
    rows, width = cot.shape
    rank, features = adn.shape
    share = (features + width) // (2 * X)
    n = share // 6
    scratch = [
        pltpu.VMEM((2 * X, 2, rows // 2, width), BF16),
        pltpu.VMEM((Z, 2, 2, rows // 2, width), BF16),
        pltpu.VMEM((Z, 2 * X, rows, 2 * rows), BF16),
        pltpu.VMEM((rows, features), BF16),
        pltpu.VMEM((rows, width), BF16),
        pltpu.VMEM((rank, features), BF16),
        pltpu.VMEM((rank, width), BF16),
        pltpu.VMEM((4, 2 * rows, rank), BF16),
        pltpu.VMEM((X, rank, share), F32),
        pltpu.VMEM((X, rank, share), BF16),
        pltpu.VMEM((X, rank, share), BF16),
        pltpu.VMEM((X, rank, share), BF16),
        pltpu.VMEM((X - 1, rank, share), BF16),
        pltpu.VMEM((2, rank, share // 2), F32),
        pltpu.VMEM((2 * X, 8, 128), F32),
        pltpu.VMEM((rank, share // 2), F32),
        pltpu.VMEM((rank, share // 2), F32),
        pltpu.VMEM((Z, 8, n), F32),
        pltpu.VMEM((Z - 1, 8, n), F32),
        pltpu.VMEM((X, 8, n), F32),
        pltpu.VMEM((Z, X, 8, n), F32),
        pltpu.VMEM((2, 6, X, 8, n), F32),
        pltpu.VMEM((2, 2, 6, X, 8, n), F32),
        pltpu.VMEM((rank, features), F32),
        pltpu.VMEM((rank, width), F32),
        pltpu.SemaphoreType.DMA((13,)),
        pltpu.SemaphoreType.DMA((TOTAL,)),
    ]
    anywhere = pl.BlockSpec(memory_space=pl.ANY)
    hbm = pl.BlockSpec(memory_space=pltpu.HBM)
    return pl.pallas_call(
        body,
        out_shape=(
            jax.ShapeDtypeStruct((rows, features), BF16),
            jax.ShapeDtypeStruct((rank, features), F32),
            jax.ShapeDtypeStruct((rank, width), F32),
        ),
        in_specs=[pl.BlockSpec(memory_space=pltpu.SMEM)] + [hbm] * 5,
        out_specs=(anywhere, anywhere, anywhere),
        scratch_shapes=scratch,
        compiler_params=pltpu.CompilerParams(
            collective_id=0, has_side_effects=True, vmem_limit_bytes=44 << 20
        ),
    )(lengths, *(pltpu.with_memory_space_constraint(a, pltpu.HBM) for a in (inp, cot, frz, adn, aup)))


def close(lengths, raw, gd, gu, og_out, gd_out, gu_out, masked, sem):
    copies = [
        pltpu.make_async_copy(gd, gd_out, sem.at[0]),
        pltpu.make_async_copy(gu, gu_out, sem.at[1]),
    ]
    rows = raw.shape[0]
    n = masked.shape[1]
    for i in range(rows // n):
        at = pl.ds(i * n, n)
        position = lax.axis_index("ctx") * rows + i * n
        position = position + lax.broadcasted_iota(jnp.int32, (n, 1), 0)
        masked[i] = jnp.where(position < lengths[0], raw[at, :], jnp.zeros((), BF16))
        copies.append(pltpu.make_async_copy(masked.at[i], og_out.at[at], sem.at[2 + i]))
        copies[-1].start()
        if i == 0:
            for copy in copies[:2]:
                copy.start()
    for copy in copies:
        copy.wait()


def shard(inputs, cotangent, lengths, frozen, adapter_down, adapter_up):
    _, rows, features = inputs.shape
    results = fused(lengths, inputs[0], cotangent[0], frozen, adapter_down, adapter_up)
    vmem = pl.BlockSpec(memory_space=pltpu.VMEM)
    hbm = pl.BlockSpec(memory_space=pltpu.HBM)
    n = 16
    input_grads, grad_down, grad_up = pl.pallas_call(
        close,
        out_shape=[jax.ShapeDtypeStruct(r.shape, r.dtype) for r in results],
        in_specs=[pl.BlockSpec(memory_space=pltpu.SMEM)] + [vmem] * 3,
        out_specs=[hbm] * 3,
        scratch_shapes=[
            pltpu.VMEM((rows // n, n, features), BF16),
            pltpu.SemaphoreType.DMA((2 + rows // n,)),
        ],
        compiler_params=pltpu.CompilerParams(vmem_limit_bytes=16 << 20),
    )(lengths, *results)
    return input_grads[None], grad_down, grad_up


def solution(mesh):
    rows = P(("dp", "fsdp"), "ctx", None)
    return jax.shard_map(
        shard,
        mesh=mesh,
        in_specs=(rows, rows, P(("dp", "fsdp")), P(("fsdp", "ctx"), None), P(), P()),
        out_specs=(rows, P(), P()),
        check_vma=False,
    )
```
